32 devices in a mesh: row: 4 (over z), col: 8 (over y, x, core).
Axes of the slice: x: 2, y: 2, z: 4, core: 2. Of those that a mesh axis runs over, the one named last changes fastest.
Arguments:
- child_inverse: bfloat16 [28672, 14336], P('row', 'col'), as said below
- root_upper: bfloat16 [20480, 20480], P('row', 'col'), as said below
- coupling: bfloat16 [4096, 28672], P('col', 'row'), may hold values from -0.046875 to 0.046875
- child_rhs: float32 [14336, 2, 128], P('col'), may hold values from -6 to 6
- root_rhs: float32 [20480, 128], P(('row', 'col')), may hold values from -6 to 6
- child_map: int32 [2, 32], replicated, may hold values from 0 to 159, as said below
Outputs:
- root_solution: float32 [20480, 128], P(('row', 'col'))
- child_solution: float32 [14336, 2, 128], P('col')
The draws below stay inside these ranges and needn't reach their ends.
Inputs may be any that keep to these rules, and one draw needn't show every extreme that they name: `child_inverse`: for each child k, rows k * 14336 to (k + 1) * 14336 - 1 hold a lower triangular matrix: zero above the diagonal, diagonal entries between 0.5 and 1.5. `root_upper`: an upper triangular matrix: zero below the diagonal, diagonal entries between 0.5 and 1.5. `child_map`: each row lists 4096 / 128 distinct root blocks in increasing order, beginning with block 0 and ending with block 159.
All inputs are finite; a program needn't handle non-finite values.
Results may differ from the reference program's by a relative error of at most 0.018.
Values may be sent and summed in bfloat16 or wider, within the bound.
A program may use at most 192 MiB of HBM per device.

```python
import math
import jax
import jax.numpy as jnp
from jax import lax

S0 = 20480
S1 = 14336
U = 4096
NRHS = 128
BLK = 128


def triangle_draw(key, shape, order, lower):
    noise_key = jax.random.fold_in(key, 11)
    diag_key = jax.random.fold_in(key, 12)
    row_ids = lax.broadcasted_iota(jnp.int32, shape, 0) % order
    col_ids = lax.broadcasted_iota(jnp.int32, shape, 1)
    noise = jax.random.normal(noise_key, shape, jnp.float32)
    noise = noise * (1.0 / math.sqrt(order))
    diagonal = jax.random.uniform(diag_key, (shape[0], 1), jnp.float32, 0.5, 1.5)
    if lower:
        inside = row_ids > col_ids
    else:
        inside = row_ids < col_ids
    return jnp.where(inside, noise, jnp.where(row_ids == col_ids, diagonal, 0.0))


def draw_child_inverse(key, part):
    return triangle_draw(key, (2 * S1, S1), S1, True).astype(jnp.bfloat16)


def draw_root_upper(key, part):
    return triangle_draw(key, (S0, S0), S0, False).astype(jnp.bfloat16)


def draw_child_map(key, part):
    map_rows = []
    for member in range(2):
        middle = jax.random.permutation(jax.random.fold_in(key, 21 + member), S0 // BLK - 2)[:U // BLK - 2] + 1
        ordered = jnp.sort(middle.astype(jnp.int32))
        first_block = jnp.zeros((1,), jnp.int32)
        last_block = jnp.full((1,), S0 // BLK - 1, jnp.int32)
        map_rows.append(jnp.concatenate([first_block, ordered, last_block]))
    return jnp.stack(map_rows)


def block_levels(stream_key, dims, split, smallest, top_value):
    gain = 1.0
    for dim, parts in split:
        steps = jax.random.uniform(jax.random.fold_in(jax.random.fold_in(stream_key, 6), dim), (parts,), jnp.float32, smallest / len(split), top_value / len(split))
        gain = gain * jnp.repeat(jnp.exp(steps), dims[dim] // parts).reshape((-1,) + (1,) * (len(dims) - 1 - dim))
    return gain


def scatter_about(key, shape, spread, most, pieces=(), dtype=jnp.bfloat16):
    drawn = jax.random.normal(key, shape, jnp.float32) * spread
    if len(pieces) > 0:
        drawn = block_levels(key, shape, pieces, -0.22, 0.18) * drawn
    return jnp.clip(drawn, min=-most, max=most).astype(dtype)


def setup_inputs(seed: int = 0) -> dict:
    key_of = jax.random.split(jax.random.key(seed), 7)
    child_inverse = draw_child_inverse(jax.random.fold_in(key_of[6], 71), 0)
    root_upper = draw_root_upper(jax.random.fold_in(key_of[6], 71), 0)
    coupling = scatter_about(key_of[2], (U, 2 * S1), S1 ** -0.5, 0.046875, ((0, 8), (1, 4)))
    child_rhs = scatter_about(key_of[3], (S1, 2, NRHS), 1.0, 6.0, ((0, 8),), jnp.float32)
    root_rhs = scatter_about(key_of[4], (S0, NRHS), 1.0, 6.0, ((0, 32),), jnp.float32)
    child_map = draw_child_map(jax.random.fold_in(key_of[6], 71), 0)
    return dict(child_inverse=child_inverse, root_upper=root_upper, coupling=coupling, child_rhs=child_rhs, root_rhs=root_rhs, child_map=child_map)


def reference(child_inverse, root_upper, coupling, child_rhs, root_rhs, child_map):
    rhs_low = child_rhs.astype(jnp.bfloat16)
    root_blocks = S0 // BLK
    update_sum = jnp.zeros((root_blocks, BLK, NRHS), jnp.float32)
    solved_list = []
    for member in range(2):
        inverse = child_inverse[member * S1:(member + 1) * S1]
        part_coupling = coupling[:, member * S1:(member + 1) * S1]
        child_solved = jnp.dot(inverse, rhs_low[:, member, :], preferred_element_type=jnp.float32)
        update = jnp.dot(part_coupling, child_solved.astype(jnp.bfloat16), preferred_element_type=jnp.float32)
        update_sum = update_sum.at[child_map[member]].add(update.reshape(U // BLK, BLK, NRHS))
        solved_list.append(child_solved)
    root_changed = root_rhs - update_sum.reshape(S0, NRHS)
    root_low = root_changed.astype(jnp.bfloat16)
    root_solved = jnp.dot(root_upper.T, root_low, preferred_element_type=jnp.float32)
    solved_low = root_solved.astype(jnp.bfloat16)
    root_solution = jnp.dot(root_upper, solved_low, preferred_element_type=jnp.float32)
    rows_low = root_solution.astype(jnp.bfloat16).reshape(root_blocks, BLK, NRHS)
    final_list = []
    for member in range(2):
        inverse = child_inverse[member * S1:(member + 1) * S1]
        part_coupling = coupling[:, member * S1:(member + 1) * S1]
        picked = rows_low[child_map[member]].reshape(U, NRHS)
        back_term = jnp.dot(part_coupling.T, picked, preferred_element_type=jnp.float32)
        adjusted = (solved_list[member] - back_term).astype(jnp.bfloat16)
        final_list.append(jnp.dot(inverse.T, adjusted, preferred_element_type=jnp.float32))
    return root_solution, jnp.stack(final_list, axis=1)
```

```python
import functools

import jax
import jax.numpy as jnp
from jax import lax
from jax.experimental import pallas as pl
from jax.experimental.pallas import tpu as pltpu
from jax.sharding import PartitionSpec as P

BLK = 128
MESH = pl.DeviceIdType.MESH
VMEM = 56 * 2**20


def bits_of(n):
    m = n.bit_length() - 1
    assert 1 << m == n
    return m


def greet(axis, me, bits):
    barrier = pltpu.get_barrier_semaphore()
    for b in bits:
        pl.semaphore_signal(
            barrier, inc=1, device_id={axis: me ^ (1 << b)}, device_id_type=MESH
        )
    pl.semaphore_wait(barrier, len(bits))


def remote(axis, me, bit, src, dst, send, recv):
    copy = pltpu.make_async_remote_copy(
        src_ref=src,
        dst_ref=dst,
        send_sem=send,
        recv_sem=recv,
        device_id={axis: me ^ (1 << bit)},
        device_id_type=MESH,
    )
    copy.start()
    return copy


def run_streams(streams, steps, begin, finish):
    copies = [[begin(s, 0)] for s in range(streams)]
    for t in range(steps):
        for s in range(streams):
            copies[s][t].wait_recv()
            finish(s, t)
            if t + 1 < steps:
                copies[s].append(begin(s, t + 1))
    for own in copies:
        for copy in own:
            copy.wait_send()


def spans(me, order, n):
    low = jnp.int32(0)
    size = n
    offset = 0
    out = []
    for b in order:
        half = size // 2
        mine = (me >> b) & 1
        keep, away = low + mine * half, low + (1 - mine) * half
        out.append((keep, away, half, offset))
        low, size, offset = keep, half, offset + half
    return out


def add_landed(s, span, src, r_ref, put):
    keep, _, half, offset = span

    def add(i, _):
        total = src[s, keep + i].astype(jnp.float32) + r_ref[s, offset + i].astype(jnp.float32)
        put(keep + i, total.astype(jnp.bfloat16))
        return 0

    lax.fori_loop(0, half, add, 0)


def all_sum_kernel(axis, n, orders, gathers, x_ref, o_ref, w_ref, r_ref, send, recv):
    me = lax.axis_index(axis)
    steps = len(orders[0])
    plans = [spans(me, order, n) for order in orders]
    greet(axis, me, list(range(steps)))

    def begin(s, t):
        if t < steps:
            _, away, half, offset = plans[s][t]
            src = (x_ref if t == 0 else w_ref).at[s, pl.ds(away, half)]
            dst = r_ref.at[s, pl.ds(offset, half)]
            bit = orders[s][t]
        else:
            back = 2 * steps - 1 - t
            src = dst = o_ref.at[s, pl.ds(plans[s][back][0], plans[s][back][2])]
            bit = orders[s][back]
        return remote(axis, me, bit, src, dst, send.at[s, t], recv.at[s, t])

    def finish(s, t):
        if t < steps:

            def put(place, value):
                if t == steps - 1:
                    o_ref[s, place] = value
                else:
                    w_ref[s, place] = value

            add_landed(s, plans[s][t], x_ref if t == 0 else w_ref, r_ref, put)

    run_streams(len(orders), steps + gathers, begin, finish)


def all_sum(x, axis, n, orders, cid, gathers=None):
    rows, width = x.shape
    m = bits_of(n)
    gathers = m if gathers is None else gathers
    streams = len(orders)
    shape = (streams, n, rows // (streams * n), width)
    out = pl.pallas_call(
        functools.partial(all_sum_kernel, axis, n, orders, gathers),
        out_shape=jax.ShapeDtypeStruct(shape, jnp.bfloat16),
        in_specs=[pl.BlockSpec(memory_space=pltpu.VMEM)],
        out_specs=pl.BlockSpec(memory_space=pltpu.VMEM),
        scratch_shapes=[
            pltpu.VMEM(shape, jnp.bfloat16),
            pltpu.VMEM(shape, jnp.bfloat16),
            pltpu.SemaphoreType.DMA((streams, 2 * m)),
            pltpu.SemaphoreType.DMA((streams, 2 * m)),
        ],
        compiler_params=pltpu.CompilerParams(collective_id=cid, has_side_effects=True),
    )(x.reshape(shape))
    return out.reshape(rows, width)


def both_sum_kernel(axis, n, streams, x_ref, o_ref, w_ref, r_ref, send, recv):
    me = lax.axis_index(axis)
    m = bits_of(n)
    slot = me >> (m - 1)
    plan = spans(me, list(range(m - 1)), n // 2)
    greet(axis, me, list(range(m)))

    def begin(s, t):
        if t < m - 1:
            _, away, half, offset = plan[t]
            src = (x_ref if t == 0 else w_ref).at[s, pl.ds(away, half)]
            dst = r_ref.at[s, pl.ds(offset, half)]
            bit = t
        elif t == m - 1:
            src = dst = o_ref.at[slot, s, pl.ds(plan[-1][0], 1)]
            bit = m - 1
        else:
            bit = 2 * (m - 1) - t
            src = dst = o_ref.at[:, s, pl.ds(plan[bit][0], plan[bit][2])]
        return remote(axis, me, bit, src, dst, send.at[s, t], recv.at[s, t])

    def finish(s, t):
        if t < m - 1:

            def put(place, value):
                if t == m - 2:
                    o_ref[slot, s, place] = value
                else:
                    w_ref[s, place] = value

            add_landed(s, plan[t], x_ref if t == 0 else w_ref, r_ref, put)

    run_streams(streams, 2 * m - 1, begin, finish)


def both_sum(x, axis, n, streams, cid):
    rows, width = x.shape
    m = bits_of(n)
    half = n // 2
    shape = (streams, half, rows // (streams * half), width)
    out = pl.pallas_call(
        functools.partial(both_sum_kernel, axis, n, streams),
        out_shape=jax.ShapeDtypeStruct((2,) + shape, jnp.bfloat16),
        in_specs=[pl.BlockSpec(memory_space=pltpu.VMEM)],
        out_specs=pl.BlockSpec(memory_space=pltpu.VMEM),
        scratch_shapes=[
            pltpu.VMEM(shape, jnp.bfloat16),
            pltpu.VMEM(shape, jnp.bfloat16),
            pltpu.SemaphoreType.DMA((streams, 2 * m)),
            pltpu.SemaphoreType.DMA((streams, 2 * m)),
        ],
        compiler_params=pltpu.CompilerParams(collective_id=cid, has_side_effects=True),
    )(x.reshape(shape))
    return out.reshape(2, rows, width)


def place_kernel(idx_ref, update_ref, given_ref, o_ref):
    def body(j, _):
        value = given_ref[j]
        for k in range(2):
            i = idx_ref[k, j]
            block = update_ref[jnp.maximum(i, 0)].astype(jnp.float32)
            value = value - jnp.where(i >= 0, block, 0.0)
        o_ref[j] = value.astype(jnp.bfloat16)
        return 0

    lax.fori_loop(0, o_ref.shape[0], body, 0)


def pick_kernel(idx_ref, rows_ref, o_ref):
    def body(j, _):
        i = idx_ref[j]
        block = rows_ref[jnp.maximum(i, 0)].astype(jnp.float32)
        o_ref[j] = jnp.where(i >= 0, block, 0.0).astype(jnp.bfloat16)
        return 0

    lax.fori_loop(0, o_ref.shape[0], body, 0)


def weave_kernel(x_ref, o_ref):
    step = 64

    def body(i, _):
        rows = pl.ds(pl.multiple_of(i * step, step), step)
        for k in range(2):
            o_ref[rows, k, :] = x_ref[k, rows, :].astype(jnp.float32)
        return 0

    lax.fori_loop(0, o_ref.shape[0] // step, body, 0)


CHUNK = 512
FAR = (0, 2, 5, 8, 11, 14, 16)


class PlaneSum:
    def __init__(self, me, chunks, w_ref, r_ref, o_ref, send, recv):
        self.me, self.chunks = me, chunks
        self.w, self.r, self.o = w_ref, r_ref, o_ref
        self.send, self.recv = send, recv

    def bits(self, j):
        first = 1 + j % 2
        return 0, first, 3 - first

    def keeps(self, j):
        low, size, out = 0, CHUNK, []
        for b in self.bits(j):
            size = size // 2
            mine = (self.me >> b) & 1
            out.append((low + mine * size, low + (1 - mine) * size, size))
            low = low + mine * size
        return out

    def copy(self, s, j):
        bits, keeps = self.bits(j), self.keeps(j)
        if s < 3:
            _, away, size = keeps[s]
            src = self.w.at[j, pl.ds(pl.multiple_of(away, size), size)]
            dst = self.r.at[j, pl.ds(CHUNK - 2 * size, size)]
            bit = bits[s]
        else:
            keep, _, size = keeps[5 - s]
            src = dst = self.o.at[j, pl.ds(pl.multiple_of(keep, size), size)]
            bit = bits[5 - s]
        return pltpu.make_async_remote_copy(
            src_ref=src,
            dst_ref=dst,
            send_sem=self.send.at[s, j],
            recv_sem=self.recv.at[s, j],
            device_id={"col": self.me ^ (1 << bit)},
            device_id_type=MESH,
        )

    def total(self, s, j, low, size):
        keep, _, half = self.keeps(j)[s]
        mine = self.w[j, pl.ds(pl.multiple_of(keep + low, size), size)].astype(jnp.float32)
        landed = self.r[j, pl.ds(pl.multiple_of(CHUNK - 2 * half + low, size), size)]
        return mine + landed.astype(jnp.float32)

    def fold(self, s, j):
        self.copy(s, j).wait_recv()
        keep, _, half = self.keeps(j)[s]
        size = half // 2
        stay = ((self.me >> self.bits(j)[s + 1]) & 1) * size
        for low, last in ((size - stay, False), (stay, True)):
            self.w[j, pl.ds(pl.multiple_of(keep + low, size), size)] = self.total(
                s, j, low, size
            ).astype(jnp.bfloat16)
            if not last:
                self.copy(s + 1, j).start()

    def run(self, produce, own, consume, lags=FAR):
        def stage(k, j):
            if k == 0:
                self.w[j] = produce(j)
                self.copy(0, j).start()
            elif k < 3:
                self.fold(k - 1, j)
            elif k == 3:
                self.copy(2, j).wait_recv()
                keep, _, size = self.keeps(j)[2]
                place = pl.ds(pl.multiple_of(keep, size), size)
                self.o[j, place] = own(j, place, self.total(2, j, 0, size)).astype(jnp.bfloat16)
                self.copy(3, j).start()
            else:
                self.copy(k - 1, j).wait_recv()
                if k < 6:
                    self.copy(k, j).start()
                else:
                    consume(j)

        def tick(t, _):
            for k in reversed(range(7)):
                j = t - lags[k]
                pl.when((j >= 0) & (j < self.chunks))(functools.partial(stage, k, j))
            return 0

        lax.fori_loop(0, self.chunks + lags[-1], tick, 0)

        def settle(j, _):
            for s in range(6):
                self.copy(s, j).wait_send()
            return 0

        lax.fori_loop(0, self.chunks, settle, 0)


def plane_scratch(chunks, with_out):
    out = [
        pltpu.VMEM((chunks, CHUNK, BLK), jnp.bfloat16),
        pltpu.VMEM((chunks, CHUNK, BLK), jnp.bfloat16),
    ]
    if with_out:
        out.append(pltpu.VMEM((chunks, CHUNK, BLK), jnp.bfloat16))
    return out + [pltpu.SemaphoreType.DMA((6, chunks)), pltpu.SemaphoreType.DMA((6, chunks))]


def enter(partners):
    barrier = pltpu.get_barrier_semaphore()
    for partner in partners:
        pl.semaphore_signal(barrier, inc=1, device_id=partner, device_id_type=MESH)
    pl.semaphore_wait(barrier, len(partners))


AHEAD = 5


def down_kernel(
    chunks, inverse_ref, coupling_ref, rhs_ref, low_ref, update_ref,
    a_ref, c_ref, acc_ref, w_ref, r_ref, send, recv, a_sem, c_sem,
):
    me = lax.axis_index("col")

    def load(j):
        return pltpu.make_async_copy(
            inverse_ref.at[pl.ds(pl.multiple_of(j * CHUNK, CHUNK), CHUNK)],
            a_ref.at[j],
            a_sem.at[j],
        )

    for j in range(AHEAD):
        load(j).start()
    enter([{"col": me ^ (1 << b)} for b in range(3)])
    acc_ref[...] = jnp.zeros_like(acc_ref)
    whole = pltpu.make_async_copy(coupling_ref, c_ref, c_sem)

    def produce(j):
        load(j).wait()

        @pl.when(j + AHEAD < chunks)
        def _():
            load(j + AHEAD).start()

        @pl.when(j + AHEAD == chunks)
        def _():
            whole.start()

        return jnp.dot(a_ref[j], rhs_ref[...], preferred_element_type=jnp.float32).astype(
            jnp.bfloat16
        )

    def consume(j):
        @pl.when(j == 0)
        def _():
            whole.wait()

        columns = pl.ds(pl.multiple_of(j * CHUNK, CHUNK), CHUNK)
        acc_ref[...] += jnp.dot(
            c_ref[:, columns], low_ref[j], preferred_element_type=jnp.float32
        )

    PlaneSum(me, chunks, w_ref, r_ref, low_ref, send, recv).run(
        produce, lambda j, place, value: value, consume
    )
    update_ref[...] = acc_ref[...].astype(jnp.bfloat16)


def down(child_inverse, coupling, own_rhs, cid):
    rows, depth = child_inverse.shape
    chunks = rows // CHUNK
    coupled = coupling.shape[0]
    vmem = pl.BlockSpec(memory_space=pltpu.VMEM)
    anywhere = pl.BlockSpec(memory_space=pl.ANY)
    low, update = pl.pallas_call(
        functools.partial(down_kernel, chunks),
        out_shape=(
            jax.ShapeDtypeStruct((chunks, CHUNK, BLK), jnp.bfloat16),
            jax.ShapeDtypeStruct((coupled, BLK), jnp.bfloat16),
        ),
        in_specs=[anywhere, anywhere, vmem],
        out_specs=(vmem, vmem),
        scratch_shapes=[
            pltpu.VMEM((chunks, CHUNK, depth), jnp.bfloat16),
            pltpu.VMEM((coupled, rows), jnp.bfloat16),
            pltpu.VMEM((coupled, BLK), jnp.float32),
        ]
        + plane_scratch(chunks, False)
        + [pltpu.SemaphoreType.DMA((chunks,)), pltpu.SemaphoreType.DMA],
        compiler_params=pltpu.CompilerParams(
            collective_id=cid, has_side_effects=True, vmem_limit_bytes=VMEM
        ),
    )(child_inverse, coupling, own_rhs)
    return low, update


def local(row_devices, col_devices, child_inverse, root_upper, coupling, child_rhs, root_rhs, child_map):
    row_place = lax.axis_index("row")
    col_place = lax.axis_index("col")
    child_slot = row_place // (row_devices // 2)
    root_rows = root_upper.shape[0]
    coupled = coupling.shape[0]
    rhs_width = child_rhs.shape[2]
    vmem = pl.BlockSpec(memory_space=pltpu.VMEM)
    smem = pl.BlockSpec(memory_space=pltpu.SMEM)
    row_bits = list(range(bits_of(row_devices)))
    col_bits = list(range(bits_of(col_devices)))
    col_orders = [col_bits, col_bits[:1] + col_bits[:0:-1]] * 2
    row_orders = [row_bits, row_bits[::-1]] * 2
    pick_order = [row_bits[-1:] + row_bits[:-1]]
    contract_first = (((0,), (0,)), ((), ()))

    per_col = coupled // BLK
    root_blocks = root_rows // BLK
    local_map = lax.dynamic_slice_in_dim(child_map, col_place * per_col, per_col, 1)
    target = local_map - row_place * root_blocks
    block_hits = target[:, :, None] == jnp.arange(root_blocks, dtype=jnp.int32)[None, None, :]
    slots = jnp.arange(2 * per_col, dtype=jnp.int32).reshape(2, per_col, 1)
    place_idx = jnp.max(jnp.where(block_hits, slots, -1), axis=1)
    pick_idx = jnp.where((target >= 0) & (target < root_blocks), target, -1).reshape(-1)
    rhs_rows = root_rhs.shape[0]
    given_rows = lax.dynamic_update_slice(
        jnp.zeros((root_rows, rhs_width), jnp.float32),
        root_rhs,
        (col_place * rhs_rows, jnp.int32(0)),
    )

    own_rhs = lax.dynamic_index_in_dim(child_rhs, child_slot, 1, keepdims=False).astype(
        jnp.bfloat16
    )
    child_low = all_sum(
        jnp.dot(child_inverse, own_rhs, preferred_element_type=jnp.float32).astype(jnp.bfloat16),
        "col", col_devices, col_orders, 0,
    )
    update = jnp.dot(coupling, child_low, preferred_element_type=jnp.float32)
    update_both = both_sum(update.astype(jnp.bfloat16), "row", row_devices, 2, 1)
    root_term = pl.pallas_call(
        place_kernel,
        out_shape=jax.ShapeDtypeStruct((root_blocks, BLK, rhs_width), jnp.bfloat16),
        in_specs=[smem, vmem, vmem],
        out_specs=vmem,
    )(
        place_idx,
        update_both.reshape(2 * per_col, BLK, rhs_width),
        given_rows.reshape(root_blocks, BLK, rhs_width),
    )
    root_low = all_sum(
        root_term.reshape(root_rows, rhs_width), "col", col_devices, col_orders, 2
    )
    solved_low = all_sum(
        lax.dot_general(
            root_upper, root_low, contract_first, preferred_element_type=jnp.float32
        ).astype(jnp.bfloat16),
        "row", row_devices, row_orders, 3,
    )
    rows_low = all_sum(
        jnp.dot(root_upper, solved_low, preferred_element_type=jnp.float32).astype(jnp.bfloat16),
        "col", col_devices, col_orders, 4,
    )
    root_solution = lax.dynamic_slice_in_dim(rows_low, col_place * rhs_rows, rhs_rows, 0).astype(
        jnp.float32
    )
    picked = pl.pallas_call(
        pick_kernel,
        out_shape=jax.ShapeDtypeStruct((2 * per_col, BLK, rhs_width), jnp.bfloat16),
        in_specs=[smem, vmem],
        out_specs=vmem,
    )(pick_idx, rows_low.reshape(root_blocks, BLK, rhs_width))
    picked_half = all_sum(
        picked.reshape(2 * coupled, rhs_width), "row", row_devices, pick_order, 5,
        gathers=len(row_bits) - 1,
    )
    own_pick = lax.dynamic_slice_in_dim(picked_half, child_slot * coupled, coupled, 0)
    back_term = all_sum(
        lax.dot_general(
            coupling, own_pick, contract_first, preferred_element_type=jnp.float32
        ).astype(jnp.bfloat16),
        "col", col_devices, col_orders, 6,
    )
    adjusted = (child_low.astype(jnp.float32) - back_term.astype(jnp.float32)).astype(
        jnp.bfloat16
    )
    final_rows = lax.dot_general(
        child_inverse, adjusted, contract_first, preferred_element_type=jnp.float32
    )
    final_both = both_sum(final_rows.astype(jnp.bfloat16), "row", row_devices, 4, 7)
    child_solution = pl.pallas_call(
        weave_kernel,
        out_shape=jax.ShapeDtypeStruct(child_rhs.shape, jnp.float32),
        in_specs=[vmem],
        out_specs=vmem,
    )(final_both)
    return (root_solution, child_solution)


def near(row_devices, col_devices, child_inverse, root_upper, coupling, child_rhs, root_rhs, child_map):
    row_place = lax.axis_index("row")
    col_place = lax.axis_index("col")
    child_slot = row_place // (row_devices // 2)
    root_rows = root_upper.shape[0]
    coupled = coupling.shape[0]
    rhs_width = child_rhs.shape[2]
    vmem = pl.BlockSpec(memory_space=pltpu.VMEM)
    smem = pl.BlockSpec(memory_space=pltpu.SMEM)
    row_bits = list(range(bits_of(row_devices)))
    col_bits = list(range(bits_of(col_devices)))
    col_orders = [col_bits, col_bits[:1] + col_bits[:0:-1]] * 2
    row_orders = [row_bits, row_bits[::-1]] * 2
    pick_order = [row_bits[-1:] + row_bits[:-1]]
    contract_first = (((0,), (0,)), ((), ()))

    per_col = coupled // BLK
    root_blocks = root_rows // BLK
    local_map = lax.dynamic_slice_in_dim(child_map, col_place * per_col, per_col, 1)
    target = local_map - row_place * root_blocks
    block_hits = target[:, :, None] == jnp.arange(root_blocks, dtype=jnp.int32)[None, None, :]
    slots = jnp.arange(2 * per_col, dtype=jnp.int32).reshape(2, per_col, 1)
    place_idx = jnp.max(jnp.where(block_hits, slots, -1), axis=1)
    pick_idx = jnp.where((target >= 0) & (target < root_blocks), target, -1).reshape(-1)
    rhs_rows = root_rhs.shape[0]
    given_rows = lax.dynamic_update_slice(
        jnp.zeros((root_rows, rhs_width), jnp.float32),
        root_rhs,
        (col_place * rhs_rows, jnp.int32(0)),
    )

    own_rhs = lax.dynamic_index_in_dim(child_rhs, child_slot, 1, keepdims=False).astype(
        jnp.bfloat16
    )
    child_low, update = down(child_inverse, coupling, own_rhs, 0)
    child_low = child_low.reshape(-1, rhs_width)
    update_both = both_sum(update, "row", row_devices, 2, 1)
    root_term = pl.pallas_call(
        place_kernel,
        out_shape=jax.ShapeDtypeStruct((root_blocks, BLK, rhs_width), jnp.bfloat16),
        in_specs=[smem, vmem, vmem],
        out_specs=vmem,
    )(
        place_idx,
        update_both.reshape(2 * per_col, BLK, rhs_width),
        given_rows.reshape(root_blocks, BLK, rhs_width),
    )
    root_low = all_sum(
        root_term.reshape(root_rows, rhs_width), "col", col_devices, col_orders, 2
    )
    solved_low = all_sum(
        lax.dot_general(
            root_upper, root_low, contract_first, preferred_element_type=jnp.float32
        ).astype(jnp.bfloat16),
        "row", row_devices, row_orders, 3,
    )
    rows_low = all_sum(
        jnp.dot(root_upper, solved_low, preferred_element_type=jnp.float32).astype(jnp.bfloat16),
        "col", col_devices, col_orders, 4,
    )
    root_solution = lax.dynamic_slice_in_dim(rows_low, col_place * rhs_rows, rhs_rows, 0).astype(
        jnp.float32
    )
    picked = pl.pallas_call(
        pick_kernel,
        out_shape=jax.ShapeDtypeStruct((2 * per_col, BLK, rhs_width), jnp.bfloat16),
        in_specs=[smem, vmem],
        out_specs=vmem,
    )(pick_idx, rows_low.reshape(root_blocks, BLK, rhs_width))
    picked_half = all_sum(
        picked.reshape(2 * coupled, rhs_width), "row", row_devices, pick_order, 5,
        gathers=len(row_bits) - 1,
    )
    own_pick = lax.dynamic_slice_in_dim(picked_half, child_slot * coupled, coupled, 0)
    back_term = all_sum(
        lax.dot_general(
            coupling, own_pick, contract_first, preferred_element_type=jnp.float32
        ).astype(jnp.bfloat16),
        "col", col_devices, col_orders, 6,
    )
    adjusted = (child_low.astype(jnp.float32) - back_term.astype(jnp.float32)).astype(
        jnp.bfloat16
    )
    final_rows = lax.dot_general(
        child_inverse, adjusted, contract_first, preferred_element_type=jnp.float32
    )
    final_both = both_sum(final_rows.astype(jnp.bfloat16), "row", row_devices, 4, 7)
    child_solution = pl.pallas_call(
        weave_kernel,
        out_shape=jax.ShapeDtypeStruct(child_rhs.shape, jnp.float32),
        in_specs=[vmem],
        out_specs=vmem,
    )(final_both)
    return (root_solution, child_solution)


def solution(mesh):
    body = near if (mesh.shape["row"], mesh.shape["col"]) == (4, 8) else local
    return jax.shard_map(
        functools.partial(body, mesh.shape["row"], mesh.shape["col"]),
        mesh=mesh,
        in_specs=(
            P("row", "col"),
            P("row", "col"),
            P("col", "row"),
            P("col", None, None),
            P(("row", "col"), None),
            P(),
        ),
        out_specs=(P(("row", "col"), None), P("col", None, None)),
        check_vma=False,
    )
```

```python
import functools

import jax
import jax.numpy as jnp
from jax import lax
from jax.experimental import pallas as pl
from jax.experimental.pallas import tpu as pltpu
from jax.sharding import PartitionSpec as P

BLK = 128
MESH = pl.DeviceIdType.MESH
VMEM = 58 * 2**20


def bits_of(n):
    m = n.bit_length() - 1
    assert 1 << m == n
    return m


def greet(axis, me, bits):
    barrier = pltpu.get_barrier_semaphore()
    for b in bits:
        pl.semaphore_signal(
            barrier, inc=1, device_id={axis: me ^ (1 << b)}, device_id_type=MESH
        )
    pl.semaphore_wait(barrier, len(bits))


def remote(axis, me, bit, src, dst, send, recv):
    copy = pltpu.make_async_remote_copy(
        src_ref=src,
        dst_ref=dst,
        send_sem=send,
        recv_sem=recv,
        device_id={axis: me ^ (1 << bit)},
        device_id_type=MESH,
    )
    copy.start()
    return copy


def run_streams(streams, steps, begin, finish):
    copies = [[begin(s, 0)] for s in range(streams)]
    for t in range(steps):
        for s in range(streams):
            copies[s][t].wait_recv()
            finish(s, t)
            if t + 1 < steps:
                copies[s].append(begin(s, t + 1))
    for own in copies:
        for copy in own:
            copy.wait_send()


def spans(me, order, n):
    low = jnp.int32(0)
    size = n
    offset = 0
    out = []
    for b in order:
        half = size // 2
        mine = (me >> b) & 1
        keep, away = low + mine * half, low + (1 - mine) * half
        out.append((keep, away, half, offset))
        low, size, offset = keep, half, offset + half
    return out


def add_landed(s, span, src, r_ref, put):
    keep, _, half, offset = span

    def add(i, _):
        total = src[s, keep + i].astype(jnp.float32) + r_ref[s, offset + i].astype(jnp.float32)
        put(keep + i, total.astype(jnp.bfloat16))
        return 0

    lax.fori_loop(0, half, add, 0)


def all_sum_kernel(axis, n, orders, gathers, x_ref, o_ref, w_ref, r_ref, send, recv):
    me = lax.axis_index(axis)
    steps = len(orders[0])
    plans = [spans(me, order, n) for order in orders]
    greet(axis, me, list(range(steps)))

    def begin(s, t):
        if t < steps:
            _, away, half, offset = plans[s][t]
            src = (x_ref if t == 0 else w_ref).at[s, pl.ds(away, half)]
            dst = r_ref.at[s, pl.ds(offset, half)]
            bit = orders[s][t]
        else:
            back = 2 * steps - 1 - t
            src = dst = o_ref.at[s, pl.ds(plans[s][back][0], plans[s][back][2])]
            bit = orders[s][back]
        return remote(axis, me, bit, src, dst, send.at[s, t], recv.at[s, t])

    def finish(s, t):
        if t < steps:

            def put(place, value):
                if t == steps - 1:
                    o_ref[s, place] = value
                else:
                    w_ref[s, place] = value

            add_landed(s, plans[s][t], x_ref if t == 0 else w_ref, r_ref, put)

    run_streams(len(orders), steps + gathers, begin, finish)


def all_sum(x, axis, n, orders, cid, gathers=None):
    rows, width = x.shape
    m = bits_of(n)
    gathers = m if gathers is None else gathers
    streams = len(orders)
    shape = (streams, n, rows // (streams * n), width)
    out = pl.pallas_call(
        functools.partial(all_sum_kernel, axis, n, orders, gathers),
        out_shape=jax.ShapeDtypeStruct(shape, jnp.bfloat16),
        in_specs=[pl.BlockSpec(memory_space=pltpu.VMEM)],
        out_specs=pl.BlockSpec(memory_space=pltpu.VMEM),
        scratch_shapes=[
            pltpu.VMEM(shape, jnp.bfloat16),
            pltpu.VMEM(shape, jnp.bfloat16),
            pltpu.SemaphoreType.DMA((streams, 2 * m)),
            pltpu.SemaphoreType.DMA((streams, 2 * m)),
        ],
        compiler_params=pltpu.CompilerParams(collective_id=cid, has_side_effects=True),
    )(x.reshape(shape))
    return out.reshape(rows, width)


def both_sum_kernel(axis, n, streams, x_ref, o_ref, w_ref, r_ref, send, recv):
    me = lax.axis_index(axis)
    m = bits_of(n)
    slot = me >> (m - 1)
    plan = spans(me, list(range(m - 1)), n // 2)
    greet(axis, me, list(range(m)))

    def begin(s, t):
        if t < m - 1:
            _, away, half, offset = plan[t]
            src = (x_ref if t == 0 else w_ref).at[s, pl.ds(away, half)]
            dst = r_ref.at[s, pl.ds(offset, half)]
            bit = t
        elif t == m - 1:
            src = dst = o_ref.at[slot, s, pl.ds(plan[-1][0], 1)]
            bit = m - 1
        else:
            bit = 2 * (m - 1) - t
            src = dst = o_ref.at[:, s, pl.ds(plan[bit][0], plan[bit][2])]
        return remote(axis, me, bit, src, dst, send.at[s, t], recv.at[s, t])

    def finish(s, t):
        if t < m - 1:

            def put(place, value):
                if t == m - 2:
                    o_ref[slot, s, place] = value
                else:
                    w_ref[s, place] = value

            add_landed(s, plan[t], x_ref if t == 0 else w_ref, r_ref, put)

    run_streams(streams, 2 * m - 1, begin, finish)


def both_sum(x, axis, n, streams, cid):
    rows, width = x.shape
    m = bits_of(n)
    half = n // 2
    shape = (streams, half, rows // (streams * half), width)
    out = pl.pallas_call(
        functools.partial(both_sum_kernel, axis, n, streams),
        out_shape=jax.ShapeDtypeStruct((2,) + shape, jnp.bfloat16),
        in_specs=[pl.BlockSpec(memory_space=pltpu.VMEM)],
        out_specs=pl.BlockSpec(memory_space=pltpu.VMEM),
        scratch_shapes=[
            pltpu.VMEM(shape, jnp.bfloat16),
            pltpu.VMEM(shape, jnp.bfloat16),
            pltpu.SemaphoreType.DMA((streams, 2 * m)),
            pltpu.SemaphoreType.DMA((streams, 2 * m)),
        ],
        compiler_params=pltpu.CompilerParams(collective_id=cid, has_side_effects=True),
    )(x.reshape(shape))
    return out.reshape(2, rows, width)


def place_kernel(idx_ref, update_ref, given_ref, o_ref):
    def body(j, _):
        value = given_ref[j]
        for k in range(2):
            i = idx_ref[k, j]
            block = update_ref[jnp.maximum(i, 0)].astype(jnp.float32)
            value = value - jnp.where(i >= 0, block, 0.0)
        o_ref[j] = value.astype(jnp.bfloat16)
        return 0

    lax.fori_loop(0, o_ref.shape[0], body, 0)


def pick_kernel(idx_ref, rows_ref, o_ref):
    def body(j, _):
        i = idx_ref[j]
        block = rows_ref[jnp.maximum(i, 0)].astype(jnp.float32)
        o_ref[j] = jnp.where(i >= 0, block, 0.0).astype(jnp.bfloat16)
        return 0

    lax.fori_loop(0, o_ref.shape[0], body, 0)


def weave_kernel(x_ref, o_ref):
    step = 64

    def body(i, _):
        rows = pl.ds(pl.multiple_of(i * step, step), step)
        for k in range(2):
            o_ref[rows, k, :] = x_ref[k, rows, :].astype(jnp.float32)
        return 0

    lax.fori_loop(0, o_ref.shape[0] // step, body, 0)


CHUNK = 512
FAR = (0, 2, 6, 10, 14, 18, 20)


class PlaneSum:
    def __init__(self, me, chunks, w_ref, r_ref, o_ref, send, recv):
        self.me, self.chunks = me, chunks
        self.w, self.r, self.o = w_ref, r_ref, o_ref
        self.send, self.recv = send, recv

    def bits(self, j):
        first = 1 + j % 2
        return 0, first, 3 - first

    def keeps(self, j):
        low, size, out = 0, CHUNK, []
        for b in self.bits(j):
            size = size // 2
            mine = (self.me >> b) & 1
            out.append((low + mine * size, low + (1 - mine) * size, size))
            low = low + mine * size
        return out

    def copy(self, s, j):
        bits, keeps = self.bits(j), self.keeps(j)
        if s < 3:
            _, away, size = keeps[s]
            src = self.w.at[j, pl.ds(pl.multiple_of(away, size), size)]
            dst = self.r.at[j, pl.ds(CHUNK - 2 * size, size)]
            bit = bits[s]
        else:
            keep, _, size = keeps[5 - s]
            src = dst = self.o.at[j, pl.ds(pl.multiple_of(keep, size), size)]
            bit = bits[5 - s]
        return pltpu.make_async_remote_copy(
            src_ref=src,
            dst_ref=dst,
            send_sem=self.send.at[s, j],
            recv_sem=self.recv.at[s, j],
            device_id={"col": self.me ^ (1 << bit)},
            device_id_type=MESH,
        )

    def total(self, s, j, low, size):
        keep, _, half = self.keeps(j)[s]
        mine = self.w[j, pl.ds(pl.multiple_of(keep + low, size), size)].astype(jnp.float32)
        landed = self.r[j, pl.ds(pl.multiple_of(CHUNK - 2 * half + low, size), size)]
        return mine + landed.astype(jnp.float32)

    def fold(self, s, j):
        self.copy(s, j).wait_recv()
        keep, _, half = self.keeps(j)[s]
        size = half // 2
        stay = ((self.me >> self.bits(j)[s + 1]) & 1) * size
        for low, last in ((size - stay, False), (stay, True)):
            self.w[j, pl.ds(pl.multiple_of(keep + low, size), size)] = self.total(
                s, j, low, size
            ).astype(jnp.bfloat16)
            if not last:
                self.copy(s + 1, j).start()

    def run(self, produce, own, consume, lags=FAR):
        def stage(k, j):
            if k == 0:
                self.w[j] = produce(j)
                self.copy(0, j).start()
            elif k < 3:
                self.fold(k - 1, j)
            elif k == 3:
                self.copy(2, j).wait_recv()
                keep, _, size = self.keeps(j)[2]
                place = pl.ds(pl.multiple_of(keep, size), size)
                self.o[j, place] = own(j, place, self.total(2, j, 0, size)).astype(jnp.bfloat16)
                self.copy(3, j).start()
            else:
                self.copy(k - 1, j).wait_recv()
                if k < 6:
                    self.copy(k, j).start()
                else:
                    consume(j)

        def tick(t, _):
            for k in reversed(range(7)):
                j = t - lags[k]
                pl.when((j >= 0) & (j < self.chunks))(functools.partial(stage, k, j))
            return 0

        lax.fori_loop(0, self.chunks + lags[-1], tick, 0)

        def settle(j, _):
            for s in range(6):
                self.copy(s, j).wait_send()
            return 0

        lax.fori_loop(0, self.chunks, settle, 0)


def plane_scratch(chunks, with_out):
    out = [
        pltpu.VMEM((chunks, CHUNK, BLK), jnp.bfloat16),
        pltpu.VMEM((chunks, CHUNK, BLK), jnp.bfloat16),
    ]
    if with_out:
        out.append(pltpu.VMEM((chunks, CHUNK, BLK), jnp.bfloat16))
    return out + [pltpu.SemaphoreType.DMA((6, chunks)), pltpu.SemaphoreType.DMA((6, chunks))]


def enter(partners):
    barrier = pltpu.get_barrier_semaphore()
    for partner in partners:
        pl.semaphore_signal(barrier, inc=1, device_id=partner, device_id_type=MESH)
    pl.semaphore_wait(barrier, len(partners))


AHEAD = 5


def down_kernel(
    chunks, inverse_ref, coupling_ref, rhs_ref, low_ref, update_ref,
    a_ref, c_ref, acc_ref, w_ref, r_ref, send, recv, a_sem, c_sem,
):
    me = lax.axis_index("col")

    def load(j):
        return pltpu.make_async_copy(
            inverse_ref.at[pl.ds(pl.multiple_of(j * CHUNK, CHUNK), CHUNK)],
            a_ref.at[j],
            a_sem.at[j],
        )

    for j in range(AHEAD):
        load(j).start()
    enter([{"col": me ^ (1 << b)} for b in range(3)])
    acc_ref[...] = jnp.zeros_like(acc_ref)
    whole = pltpu.make_async_copy(coupling_ref, c_ref, c_sem)

    def produce(j):
        load(j).wait()

        @pl.when(j + AHEAD < chunks)
        def _():
            load(j + AHEAD).start()

        @pl.when(j + AHEAD == chunks)
        def _():
            whole.start()

        return jnp.dot(a_ref[j], rhs_ref[...], preferred_element_type=jnp.float32).astype(
            jnp.bfloat16
        )

    def consume(j):
        @pl.when(j == 0)
        def _():
            whole.wait()

        columns = pl.ds(pl.multiple_of(j * CHUNK, CHUNK), CHUNK)
        acc_ref[...] += jnp.dot(
            c_ref[:, columns], low_ref[j], preferred_element_type=jnp.float32
        )

    PlaneSum(me, chunks, w_ref, r_ref, low_ref, send, recv).run(
        produce, lambda j, place, value: value, consume
    )
    update_ref[...] = acc_ref[...].astype(jnp.bfloat16)


def down(child_inverse, coupling, own_rhs, cid):
    rows, depth = child_inverse.shape
    chunks = rows // CHUNK
    coupled = coupling.shape[0]
    vmem = pl.BlockSpec(memory_space=pltpu.VMEM)
    anywhere = pl.BlockSpec(memory_space=pl.ANY)
    low, update = pl.pallas_call(
        functools.partial(down_kernel, chunks),
        out_shape=(
            jax.ShapeDtypeStruct((chunks, CHUNK, BLK), jnp.bfloat16),
            jax.ShapeDtypeStruct((coupled, BLK), jnp.bfloat16),
        ),
        in_specs=[anywhere, anywhere, vmem],
        out_specs=(vmem, vmem),
        scratch_shapes=[
            pltpu.VMEM((chunks, CHUNK, depth), jnp.bfloat16),
            pltpu.VMEM((coupled, rows), jnp.bfloat16),
            pltpu.VMEM((coupled, BLK), jnp.float32),
        ]
        + plane_scratch(chunks, False)
        + [pltpu.SemaphoreType.DMA((chunks,)), pltpu.SemaphoreType.DMA],
        compiler_params=pltpu.CompilerParams(
            collective_id=cid, has_side_effects=True, vmem_limit_bytes=VMEM
        ),
    )(child_inverse, coupling, own_rhs)
    return low, update


class PlaneGather:
    def __init__(self, me, ref, count, send, recv):
        self.me, self.ref, self.count, self.send, self.recv = me, ref, count, send, recv

    def copy(self, i, k, q, slot):
        far = ((0, 2), (0, 4), (2, 4), (4, 2), (0, 1), (2, 1), (4, 1), (6, 1))[i]
        low, size = ((i - 2) * (BLK // 2), BLK // 2) if i in (2, 3) else (0, BLK)
        part = self.ref.at[k, self.count * (self.me ^ far[0]) + q, pl.ds(low, size)]
        return pltpu.make_async_remote_copy(
            src_ref=part,
            dst_ref=part,
            send_sem=self.send.at[i, slot],
            recv_sem=self.recv.at[i, slot],
            device_id={"col": self.me ^ far[1]},
            device_id_type=MESH,
        )

    def begin(self, *at):
        for i in (0, 1, 4):
            self.copy(i, *at).start()

    def relay(self, *at):
        for i in (0, 1):
            self.copy(i, *at).wait_recv()
            self.copy(i + 2, *at).start()
            self.copy(i + 5, *at).start()

    def across(self, *at):
        self.copy(2, *at).wait_recv()
        self.copy(3, *at).wait_recv()
        self.copy(7, *at).start()

    def land(self, *at):
        for i in range(4, 8):
            self.copy(i, *at).wait_recv()

    def settle(self, *at):
        for i in range(8):
            self.copy(i, *at).wait_send()


def row_copy(place, flip, src, dst, send, recv):
    return pltpu.make_async_remote_copy(
        src_ref=src,
        dst_ref=dst,
        send_sem=send,
        recv_sem=recv,
        device_id={"row": place ^ flip},
        device_id_type=MESH,
    )


def f32_sum(*terms):
    total = terms[0].astype(jnp.float32)
    for term in terms[1:]:
        total = total + term.astype(jnp.float32)
    return total


PIECE = 256


def root_kernel(
    map_ref, update_ref, rhs_ref, upper_ref, rows_ref,
    u_ref, pair_ref, up_ref, given_ref, x_ref, y_ref, outer_ref, mid_ref, fin_ref, acc_ref,
    w_ref, r_ref, send, recv,
    pair_sem, cross_sem, up_send, up_recv, given_send, given_recv, line_sem, u_sem,
):
    me = lax.axis_index("col")
    place = lax.axis_index("row")
    child = place >> 1
    is_mid = ((place + 1) >> 1) == 1
    is_end = ((place + 1) >> 1) != 1
    blocks = given_ref.shape[1]
    mine = rhs_ref.shape[0] // BLK
    per = update_ref.shape[0]
    depth, width = upper_ref.shape
    loads = depth // CHUNK

    def load(i):
        rows = pl.ds(i * CHUNK, CHUNK)
        return pltpu.make_async_copy(upper_ref.at[rows], u_ref.at[rows], u_sem.at[i])

    for i in range(loads):
        load(i).start()
    enter(
        [{"col": me ^ (1 << b)} for b in range(3)] + [{"row": place ^ 1}, {"row": place ^ 3}]
    )

    def pair(q):
        return row_copy(
            place, 1, update_ref.at[q], pair_ref.at[q], pair_sem.at[0, q], pair_sem.at[1, q]
        )

    def cross(q):
        part = up_ref.at[child, per * me + q]
        return row_copy(place, 3, part, part, cross_sem.at[0, q], cross_sem.at[1, q])

    def onward(q):
        part = up_ref.at[1 - child, per * me + q]
        return row_copy(place, 1, part, part, cross_sem.at[2, q], cross_sem.at[1, q])

    for q in range(per):
        pair(q).start()
    given = PlaneGather(me, given_ref, mine, given_send, given_recv)
    for q in range(mine):
        given_ref[0, mine * me + q] = rhs_ref[pl.ds(q * BLK, BLK)].astype(jnp.bfloat16)
        given.begin(0, q, q)
    gather = PlaneGather(me, up_ref, per, up_send, up_recv)
    for q in range(per):
        pair(q).wait_recv()
        up_ref[child, per * me + q] = f32_sum(update_ref[q], pair_ref[q]).astype(jnp.bfloat16)
        pl.when(is_mid)(lambda: cross(q).start())
        gather.begin(child, q, q)
    for q in range(per):
        cross(q).wait_recv()
        pl.when(is_mid)(lambda: onward(q).start())
        gather.begin(1 - child, q, per + q)
        gather.relay(child, q, q)
    for q in range(mine):
        given.relay(0, q, q)
    for q in range(per):
        gather.relay(1 - child, q, per + q)
        gather.across(child, q, q)
    for q in range(mine):
        given.across(0, q, q)
    for q in range(per):
        gather.across(1 - child, q, per + q)
    for q in range(mine):
        given.land(0, q, q)
    for q in range(per):
        gather.land(child, q, q)
        gather.land(1 - child, q, per + q)

    def put(j, _):
        value = given_ref[0, j].astype(jnp.float32)
        for k in range(2):
            i = map_ref[k, j]
            block = up_ref[k, jnp.maximum(i, 0)].astype(jnp.float32)
            value = value - jnp.where(i >= 0, block, 0.0)
        x_ref[:, pl.ds(pl.multiple_of(j * BLK, BLK), BLK)] = value.T.astype(jnp.bfloat16)
        return 0

    lax.fori_loop(0, blocks, put, 0)

    pieces = width // PIECE
    half = PIECE // 2
    own = pl.ds(pl.multiple_of(child * half, half), half)
    rest = pl.ds(pl.multiple_of((1 - child) * half, half), half)

    def line(i, p):
        if i == 0:
            src, dst, flip = y_ref.at[p], outer_ref.at[p], 1
        elif i == 1:
            src, dst, flip = y_ref.at[p, rest], mid_ref.at[p], 3
        else:
            src = dst = fin_ref.at[p, rest if i == 4 else own]
            flip = 3 if i == 2 else 1
        return row_copy(place, flip, src, dst, line_sem.at[0, i, p], line_sem.at[1, i, p])

    for i in range(loads):
        load(i).wait()
    def tile(t):
        columns = pl.ds(pl.multiple_of(t * CHUNK, CHUNK), CHUNK)
        out = jnp.dot(x_ref[...], u_ref[:, columns], preferred_element_type=jnp.float32)
        out = out.T.astype(jnp.bfloat16)
        for i in range(CHUNK // PIECE):
            y_ref[t * (CHUNK // PIECE) + i] = out[i * PIECE : (i + 1) * PIECE]

            @pl.when(is_end)
            def _():
                line(0, t * (CHUNK // PIECE) + i).start()

    def line_stage(s, p):
        if s == 0:

            @pl.when(is_mid)
            def _():
                line(0, p).wait_recv()
                y_ref[p, rest] = f32_sum(y_ref[p, rest], outer_ref[p, rest]).astype(jnp.bfloat16)
                line(1, p).start()

        elif s == 1:

            @pl.when(is_mid)
            def _():
                line(1, p).wait_recv()
                fin_ref[p, own] = f32_sum(y_ref[p, own], outer_ref[p, own], mid_ref[p]).astype(
                    jnp.bfloat16
                )
                line(2, p).start()
                line(3, p).start()

        elif s == 2:

            @pl.when(is_mid)
            def _():
                line(2, p).wait_recv()
                line(4, p).start()

        else:

            @pl.when(is_end)
            def _():
                line(3, p).wait_recv()
                line(4, p).wait_recv()

    group = CHUNK // PIECE
    groups = width // CHUNK

    def product(j, g):
        rows = pl.ds(pl.multiple_of(j * CHUNK, CHUNK), CHUNK)
        columns = pl.ds(g * CHUNK, CHUNK)
        part = fin_ref[pl.ds(g * group, group)].reshape(CHUNK, BLK)
        return jnp.dot(u_ref[rows, columns], part, preferred_element_type=jnp.float32)

    def add_group(g):
        def body(j, _):
            value = product(j, g)
            acc_ref[j] = value if g == 0 else acc_ref[j] + value
            return 0

        lax.fori_loop(0, loads, body, 0)

    for t in range(groups):
        tile(t)
    for t in range(pieces + 3):
        for s in range(4):
            if 0 <= t - s < pieces:
                line_stage(s, t - s)
        done = t - 2
        if done > 0 and done % group == 0 and done < pieces:
            add_group(done // group - 1)

    PlaneSum(me, loads, w_ref, r_ref, rows_ref, send, recv).run(
        lambda j: (acc_ref[j] + product(j, groups - 1)).astype(jnp.bfloat16),
        lambda j, at, value: value,
        lambda j: None,
    )

    for q in range(mine):
        given.settle(0, q, q)
    for q in range(per):
        pair(q).wait_send()
        gather.settle(child, q, q)
        gather.settle(1 - child, q, per + q)

    @pl.when(is_mid)
    def _():
        for q in range(per):
            cross(q).wait_send()
            onward(q).wait_send()
        for p in range(pieces):
            for i in range(1, 5):
                line(i, p).wait_send()

    @pl.when(is_end)
    def _():
        for p in range(pieces):
            line(0, p).wait_send()


def root_part(place_idx, update, root_rhs, root_upper, cid):
    depth, width = root_upper.shape
    per = update.shape[0] // BLK
    mine = root_rhs.shape[0] // BLK
    pieces = width // PIECE
    loads = depth // CHUNK
    vmem = pl.BlockSpec(memory_space=pltpu.VMEM)
    dma = pltpu.SemaphoreType.DMA
    low = jnp.bfloat16
    return pl.pallas_call(
        root_kernel,
        out_shape=jax.ShapeDtypeStruct((loads, CHUNK, BLK), low),
        in_specs=[
            pl.BlockSpec(memory_space=pltpu.SMEM), vmem, vmem, pl.BlockSpec(memory_space=pl.ANY),
        ],
        out_specs=vmem,
        scratch_shapes=[
            pltpu.VMEM((depth, width), low),
            pltpu.VMEM((per, BLK, BLK), low),
            pltpu.VMEM((2, 8 * per, BLK, BLK), low),
            pltpu.VMEM((1, depth // BLK, BLK, BLK), low),
            pltpu.VMEM((BLK, depth), low),
            pltpu.VMEM((pieces, PIECE, BLK), low),
            pltpu.VMEM((pieces, PIECE, BLK), low),
            pltpu.VMEM((pieces, PIECE // 2, BLK), low),
            pltpu.VMEM((pieces, PIECE, BLK), low),
            pltpu.VMEM((loads, CHUNK, BLK), jnp.float32),
        ]
        + plane_scratch(loads, False)
        + [
            dma((2, per)), dma((3, per)), dma((8, 2 * per)), dma((8, 2 * per)),
            dma((8, mine)), dma((8, mine)), dma((2, 5, pieces)), dma((loads,)),
        ],
        compiler_params=pltpu.CompilerParams(
            collective_id=cid, has_side_effects=True, vmem_limit_bytes=VMEM
        ),
    )(place_idx, update.reshape(per, BLK, BLK), root_rhs, root_upper)


def local(row_devices, col_devices, child_inverse, root_upper, coupling, child_rhs, root_rhs, child_map):
    row_place = lax.axis_index("row")
    col_place = lax.axis_index("col")
    child_slot = row_place // (row_devices // 2)
    root_rows = root_upper.shape[0]
    coupled = coupling.shape[0]
    rhs_width = child_rhs.shape[2]
    vmem = pl.BlockSpec(memory_space=pltpu.VMEM)
    smem = pl.BlockSpec(memory_space=pltpu.SMEM)
    row_bits = list(range(bits_of(row_devices)))
    col_bits = list(range(bits_of(col_devices)))
    col_orders = [col_bits, col_bits[:1] + col_bits[:0:-1]] * 2
    row_orders = [row_bits, row_bits[::-1]] * 2
    pick_order = [row_bits[-1:] + row_bits[:-1]]
    contract_first = (((0,), (0,)), ((), ()))

    per_col = coupled // BLK
    root_blocks = root_rows // BLK
    local_map = lax.dynamic_slice_in_dim(child_map, col_place * per_col, per_col, 1)
    target = local_map - row_place * root_blocks
    block_hits = target[:, :, None] == jnp.arange(root_blocks, dtype=jnp.int32)[None, None, :]
    slots = jnp.arange(2 * per_col, dtype=jnp.int32).reshape(2, per_col, 1)
    place_idx = jnp.max(jnp.where(block_hits, slots, -1), axis=1)
    pick_idx = jnp.where((target >= 0) & (target < root_blocks), target, -1).reshape(-1)
    rhs_rows = root_rhs.shape[0]
    given_rows = lax.dynamic_update_slice(
        jnp.zeros((root_rows, rhs_width), jnp.float32),
        root_rhs,
        (col_place * rhs_rows, jnp.int32(0)),
    )

    own_rhs = lax.dynamic_index_in_dim(child_rhs, child_slot, 1, keepdims=False).astype(
        jnp.bfloat16
    )
    child_low = all_sum(
        jnp.dot(child_inverse, own_rhs, preferred_element_type=jnp.float32).astype(jnp.bfloat16),
        "col", col_devices, col_orders, 0,
    )
    update = jnp.dot(coupling, child_low, preferred_element_type=jnp.float32)
    update_both = both_sum(update.astype(jnp.bfloat16), "row", row_devices, 2, 1)
    root_term = pl.pallas_call(
        place_kernel,
        out_shape=jax.ShapeDtypeStruct((root_blocks, BLK, rhs_width), jnp.bfloat16),
        in_specs=[smem, vmem, vmem],
        out_specs=vmem,
    )(
        place_idx,
        update_both.reshape(2 * per_col, BLK, rhs_width),
        given_rows.reshape(root_blocks, BLK, rhs_width),
    )
    root_low = all_sum(
        root_term.reshape(root_rows, rhs_width), "col", col_devices, col_orders, 2
    )
    solved_low = all_sum(
        lax.dot_general(
            root_upper, root_low, contract_first, preferred_element_type=jnp.float32
        ).astype(jnp.bfloat16),
        "row", row_devices, row_orders, 3,
    )
    rows_low = all_sum(
        jnp.dot(root_upper, solved_low, preferred_element_type=jnp.float32).astype(jnp.bfloat16),
        "col", col_devices, col_orders, 4,
    )
    root_solution = lax.dynamic_slice_in_dim(rows_low, col_place * rhs_rows, rhs_rows, 0).astype(
        jnp.float32
    )
    picked = pl.pallas_call(
        pick_kernel,
        out_shape=jax.ShapeDtypeStruct((2 * per_col, BLK, rhs_width), jnp.bfloat16),
        in_specs=[smem, vmem],
        out_specs=vmem,
    )(pick_idx, rows_low.reshape(root_blocks, BLK, rhs_width))
    picked_half = all_sum(
        picked.reshape(2 * coupled, rhs_width), "row", row_devices, pick_order, 5,
        gathers=len(row_bits) - 1,
    )
    own_pick = lax.dynamic_slice_in_dim(picked_half, child_slot * coupled, coupled, 0)
    back_term = all_sum(
        lax.dot_general(
            coupling, own_pick, contract_first, preferred_element_type=jnp.float32
        ).astype(jnp.bfloat16),
        "col", col_devices, col_orders, 6,
    )
    adjusted = (child_low.astype(jnp.float32) - back_term.astype(jnp.float32)).astype(
        jnp.bfloat16
    )
    final_rows = lax.dot_general(
        child_inverse, adjusted, contract_first, preferred_element_type=jnp.float32
    )
    final_both = both_sum(final_rows.astype(jnp.bfloat16), "row", row_devices, 4, 7)
    child_solution = pl.pallas_call(
        weave_kernel,
        out_shape=jax.ShapeDtypeStruct(child_rhs.shape, jnp.float32),
        in_specs=[vmem],
        out_specs=vmem,
    )(final_both)
    return (root_solution, child_solution)


def near(row_devices, col_devices, child_inverse, root_upper, coupling, child_rhs, root_rhs, child_map):
    row_place = lax.axis_index("row")
    col_place = lax.axis_index("col")
    child_slot = row_place // (row_devices // 2)
    root_rows = root_upper.shape[0]
    coupled = coupling.shape[0]
    rhs_width = child_rhs.shape[2]
    vmem = pl.BlockSpec(memory_space=pltpu.VMEM)
    smem = pl.BlockSpec(memory_space=pltpu.SMEM)
    row_bits = list(range(bits_of(row_devices)))
    col_bits = list(range(bits_of(col_devices)))
    col_orders = [col_bits, col_bits[:1] + col_bits[:0:-1]] * 2
    pick_order = [row_bits[-1:] + row_bits[:-1]]
    contract_first = (((0,), (0,)), ((), ()))

    per_col = coupled // BLK
    root_blocks = root_rows // BLK
    local_map = lax.dynamic_slice_in_dim(child_map, col_place * per_col, per_col, 1)
    target = local_map - row_place * root_blocks
    block_hits = (child_map - row_place * root_blocks)[:, :, None] == jnp.arange(root_blocks, dtype=jnp.int32)[None, None, :]
    slots = jnp.arange(child_map.shape[1], dtype=jnp.int32).reshape(1, -1, 1)
    place_idx = jnp.max(jnp.where(block_hits, slots, -1), axis=1)
    pick_idx = jnp.where((target >= 0) & (target < root_blocks), target, -1).reshape(-1)
    rhs_rows = root_rhs.shape[0]

    own_rhs = lax.dynamic_index_in_dim(child_rhs, child_slot, 1, keepdims=False).astype(
        jnp.bfloat16
    )
    child_low, update = down(child_inverse, coupling, own_rhs, 0)
    child_low = child_low.reshape(-1, rhs_width)
    rows_low = root_part(place_idx, update, root_rhs, root_upper, 1).reshape(-1, rhs_width)
    root_solution = lax.dynamic_slice_in_dim(rows_low, col_place * rhs_rows, rhs_rows, 0).astype(
        jnp.float32
    )
    picked = pl.pallas_call(
        pick_kernel,
        out_shape=jax.ShapeDtypeStruct((2 * per_col, BLK, rhs_width), jnp.bfloat16),
        in_specs=[smem, vmem],
        out_specs=vmem,
    )(pick_idx, rows_low.reshape(root_blocks, BLK, rhs_width))
    picked_half = all_sum(
        picked.reshape(2 * coupled, rhs_width), "row", row_devices, pick_order, 5,
        gathers=len(row_bits) - 1,
    )
    own_pick = lax.dynamic_slice_in_dim(picked_half, child_slot * coupled, coupled, 0)
    back_term = all_sum(
        lax.dot_general(
            coupling, own_pick, contract_first, preferred_element_type=jnp.float32
        ).astype(jnp.bfloat16),
        "col", col_devices, col_orders, 6,
    )
    adjusted = (child_low.astype(jnp.float32) - back_term.astype(jnp.float32)).astype(
        jnp.bfloat16
    )
    final_rows = lax.dot_general(
        child_inverse, adjusted, contract_first, preferred_element_type=jnp.float32
    )
    final_both = both_sum(final_rows.astype(jnp.bfloat16), "row", row_devices, 4, 7)
    child_solution = pl.pallas_call(
        weave_kernel,
        out_shape=jax.ShapeDtypeStruct(child_rhs.shape, jnp.float32),
        in_specs=[vmem],
        out_specs=vmem,
    )(final_both)
    return (root_solution, child_solution)


def solution(mesh):
    body = near if (mesh.shape["row"], mesh.shape["col"]) == (4, 8) else local
    return jax.shard_map(
        functools.partial(body, mesh.shape["row"], mesh.shape["col"]),
        mesh=mesh,
        in_specs=(
            P("row", "col"),
            P("row", "col"),
            P("col", "row"),
            P("col", None, None),
            P(("row", "col"), None),
            P(),
        ),
        out_specs=(P(("row", "col"), None), P("col", None, None)),
        check_vma=False,
    )
```

```python
import functools

import jax
import jax.numpy as jnp
from jax import lax
from jax.experimental import pallas as pl
from jax.experimental.pallas import tpu as pltpu
from jax.sharding import PartitionSpec as P

BLK = 128
MESH = pl.DeviceIdType.MESH
VMEM = 58 * 2**20


def bits_of(n):
    m = n.bit_length() - 1
    assert 1 << m == n
    return m


def greet(axis, me, bits):
    barrier = pltpu.get_barrier_semaphore()
    for b in bits:
        pl.semaphore_signal(
            barrier, inc=1, device_id={axis: me ^ (1 << b)}, device_id_type=MESH
        )
    pl.semaphore_wait(barrier, len(bits))


def remote(axis, me, bit, src, dst, send, recv):
    copy = pltpu.make_async_remote_copy(
        src_ref=src,
        dst_ref=dst,
        send_sem=send,
        recv_sem=recv,
        device_id={axis: me ^ (1 << bit)},
        device_id_type=MESH,
    )
    copy.start()
    return copy


def run_streams(streams, steps, begin, finish):
    copies = [[begin(s, 0)] for s in range(streams)]
    for t in range(steps):
        for s in range(streams):
            copies[s][t].wait_recv()
            finish(s, t)
            if t + 1 < steps:
                copies[s].append(begin(s, t + 1))
    for own in copies:
        for copy in own:
            copy.wait_send()


def spans(me, order, n):
    low = jnp.int32(0)
    size = n
    offset = 0
    out = []
    for b in order:
        half = size // 2
        mine = (me >> b) & 1
        keep, away = low + mine * half, low + (1 - mine) * half
        out.append((keep, away, half, offset))
        low, size, offset = keep, half, offset + half
    return out


def add_landed(s, span, src, r_ref, put):
    keep, _, half, offset = span

    def add(i, _):
        total = src[s, keep + i].astype(jnp.float32) + r_ref[s, offset + i].astype(jnp.float32)
        put(keep + i, total.astype(jnp.bfloat16))
        return 0

    lax.fori_loop(0, half, add, 0)


def all_sum_kernel(axis, n, orders, gathers, x_ref, o_ref, w_ref, r_ref, send, recv):
    me = lax.axis_index(axis)
    steps = len(orders[0])
    plans = [spans(me, order, n) for order in orders]
    greet(axis, me, list(range(steps)))

    def begin(s, t):
        if t < steps:
            _, away, half, offset = plans[s][t]
            src = (x_ref if t == 0 else w_ref).at[s, pl.ds(away, half)]
            dst = r_ref.at[s, pl.ds(offset, half)]
            bit = orders[s][t]
        else:
            back = 2 * steps - 1 - t
            src = dst = o_ref.at[s, pl.ds(plans[s][back][0], plans[s][back][2])]
            bit = orders[s][back]
        return remote(axis, me, bit, src, dst, send.at[s, t], recv.at[s, t])

    def finish(s, t):
        if t < steps:

            def put(place, value):
                if t == steps - 1:
                    o_ref[s, place] = value
                else:
                    w_ref[s, place] = value

            add_landed(s, plans[s][t], x_ref if t == 0 else w_ref, r_ref, put)

    run_streams(len(orders), steps + gathers, begin, finish)


def all_sum(x, axis, n, orders, cid, gathers=None):
    rows, width = x.shape
    m = bits_of(n)
    gathers = m if gathers is None else gathers
    streams = len(orders)
    shape = (streams, n, rows // (streams * n), width)
    out = pl.pallas_call(
        functools.partial(all_sum_kernel, axis, n, orders, gathers),
        out_shape=jax.ShapeDtypeStruct(shape, jnp.bfloat16),
        in_specs=[pl.BlockSpec(memory_space=pltpu.VMEM)],
        out_specs=pl.BlockSpec(memory_space=pltpu.VMEM),
        scratch_shapes=[
            pltpu.VMEM(shape, jnp.bfloat16),
            pltpu.VMEM(shape, jnp.bfloat16),
            pltpu.SemaphoreType.DMA((streams, 2 * m)),
            pltpu.SemaphoreType.DMA((streams, 2 * m)),
        ],
        compiler_params=pltpu.CompilerParams(collective_id=cid, has_side_effects=True),
    )(x.reshape(shape))
    return out.reshape(rows, width)


def both_sum_kernel(axis, n, streams, x_ref, o_ref, w_ref, r_ref, send, recv):
    me = lax.axis_index(axis)
    m = bits_of(n)
    slot = me >> (m - 1)
    plan = spans(me, list(range(m - 1)), n // 2)
    greet(axis, me, list(range(m)))

    def begin(s, t):
        if t < m - 1:
            _, away, half, offset = plan[t]
            src = (x_ref if t == 0 else w_ref).at[s, pl.ds(away, half)]
            dst = r_ref.at[s, pl.ds(offset, half)]
            bit = t
        elif t == m - 1:
            src = dst = o_ref.at[slot, s, pl.ds(plan[-1][0], 1)]
            bit = m - 1
        else:
            bit = 2 * (m - 1) - t
            src = dst = o_ref.at[:, s, pl.ds(plan[bit][0], plan[bit][2])]
        return remote(axis, me, bit, src, dst, send.at[s, t], recv.at[s, t])

    def finish(s, t):
        if t < m - 1:

            def put(place, value):
                if t == m - 2:
                    o_ref[slot, s, place] = value
                else:
                    w_ref[s, place] = value

            add_landed(s, plan[t], x_ref if t == 0 else w_ref, r_ref, put)

    run_streams(streams, 2 * m - 1, begin, finish)


def both_sum(x, axis, n, streams, cid):
    rows, width = x.shape
    m = bits_of(n)
    half = n // 2
    shape = (streams, half, rows // (streams * half), width)
    out = pl.pallas_call(
        functools.partial(both_sum_kernel, axis, n, streams),
        out_shape=jax.ShapeDtypeStruct((2,) + shape, jnp.bfloat16),
        in_specs=[pl.BlockSpec(memory_space=pltpu.VMEM)],
        out_specs=pl.BlockSpec(memory_space=pltpu.VMEM),
        scratch_shapes=[
            pltpu.VMEM(shape, jnp.bfloat16),
            pltpu.VMEM(shape, jnp.bfloat16),
            pltpu.SemaphoreType.DMA((streams, 2 * m)),
            pltpu.SemaphoreType.DMA((streams, 2 * m)),
        ],
        compiler_params=pltpu.CompilerParams(collective_id=cid, has_side_effects=True),
    )(x.reshape(shape))
    return out.reshape(2, rows, width)


def place_kernel(idx_ref, update_ref, given_ref, o_ref):
    def body(j, _):
        value = given_ref[j]
        for k in range(2):
            i = idx_ref[k, j]
            block = update_ref[jnp.maximum(i, 0)].astype(jnp.float32)
            value = value - jnp.where(i >= 0, block, 0.0)
        o_ref[j] = value.astype(jnp.bfloat16)
        return 0

    lax.fori_loop(0, o_ref.shape[0], body, 0)


def pick_kernel(idx_ref, rows_ref, o_ref):
    def body(j, _):
        i = idx_ref[j]
        block = rows_ref[jnp.maximum(i, 0)].astype(jnp.float32)
        o_ref[j] = jnp.where(i >= 0, block, 0.0).astype(jnp.bfloat16)
        return 0

    lax.fori_loop(0, o_ref.shape[0], body, 0)


def weave_kernel(x_ref, o_ref):
    step = 64

    def body(i, _):
        rows = pl.ds(pl.multiple_of(i * step, step), step)
        for k in range(2):
            o_ref[rows, k, :] = x_ref[k, rows, :].astype(jnp.float32)
        return 0

    lax.fori_loop(0, o_ref.shape[0] // step, body, 0)


CHUNK = 512
FAR = (0, 2, 6, 10, 14, 18, 20)


class PlaneSum:
    def __init__(self, me, chunks, w_ref, r_ref, o_ref, send, recv):
        self.me, self.chunks = me, chunks
        self.w, self.r, self.o = w_ref, r_ref, o_ref
        self.send, self.recv = send, recv

    def bits(self, j):
        first = 1 + j % 2
        return 0, first, 3 - first

    def keeps(self, j):
        low, size, out = 0, CHUNK, []
        for b in self.bits(j):
            size = size // 2
            mine = (self.me >> b) & 1
            out.append((low + mine * size, low + (1 - mine) * size, size))
            low = low + mine * size
        return out

    def copy(self, s, j):
        bits, keeps = self.bits(j), self.keeps(j)
        if s < 3:
            _, away, size = keeps[s]
            src = self.w.at[j, pl.ds(pl.multiple_of(away, size), size)]
            dst = self.r.at[j, pl.ds(CHUNK - 2 * size, size)]
            bit = bits[s]
        else:
            keep, _, size = keeps[5 - s]
            src = dst = self.o.at[j, pl.ds(pl.multiple_of(keep, size), size)]
            bit = bits[5 - s]
        return pltpu.make_async_remote_copy(
            src_ref=src,
            dst_ref=dst,
            send_sem=self.send.at[s, j],
            recv_sem=self.recv.at[s, j],
            device_id={"col": self.me ^ (1 << bit)},
            device_id_type=MESH,
        )

    def total(self, s, j, low, size):
        keep, _, half = self.keeps(j)[s]
        mine = self.w[j, pl.ds(pl.multiple_of(keep + low, size), size)].astype(jnp.float32)
        landed = self.r[j, pl.ds(pl.multiple_of(CHUNK - 2 * half + low, size), size)]
        return mine + landed.astype(jnp.float32)

    def fold(self, s, j):
        self.copy(s, j).wait_recv()
        keep, _, half = self.keeps(j)[s]
        size = half // 2
        stay = ((self.me >> self.bits(j)[s + 1]) & 1) * size
        for low, last in ((size - stay, False), (stay, True)):
            self.w[j, pl.ds(pl.multiple_of(keep + low, size), size)] = self.total(
                s, j, low, size
            ).astype(jnp.bfloat16)
            if not last:
                self.copy(s + 1, j).start()

    def run(self, produce, own, consume, lags=FAR, beside=()):
        def stage(k, j):
            if k == 0:
                self.w[j] = produce(j)
                self.copy(0, j).start()
            elif k < 3:
                self.fold(k - 1, j)
            elif k == 3:
                self.copy(2, j).wait_recv()
                keep, _, size = self.keeps(j)[2]
                place = pl.ds(pl.multiple_of(keep, size), size)
                self.o[j, place] = own(j, place, self.total(2, j, 0, size)).astype(jnp.bfloat16)
                self.copy(3, j).start()
            else:
                self.copy(k - 1, j).wait_recv()
                if k < 6:
                    self.copy(k, j).start()
                else:
                    consume(j)

        def tick(t, _):
            for k in reversed(range(7)):
                j = t - lags[k]
                pl.when((j >= 0) & (j < self.chunks))(functools.partial(stage, k, j))
            for at, act in beside:
                pl.when(t == at)(act)
            return 0

        lax.fori_loop(0, self.chunks + lags[-1], tick, 0)

        def settle(j, _):
            for s in range(6):
                self.copy(s, j).wait_send()
            return 0

        lax.fori_loop(0, self.chunks, settle, 0)


def plane_scratch(chunks, with_out):
    out = [
        pltpu.VMEM((chunks, CHUNK, BLK), jnp.bfloat16),
        pltpu.VMEM((chunks, CHUNK, BLK), jnp.bfloat16),
    ]
    if with_out:
        out.append(pltpu.VMEM((chunks, CHUNK, BLK), jnp.bfloat16))
    return out + [pltpu.SemaphoreType.DMA((6, chunks)), pltpu.SemaphoreType.DMA((6, chunks))]


def enter(partners):
    barrier = pltpu.get_barrier_semaphore()
    for partner in partners:
        pl.semaphore_signal(barrier, inc=1, device_id=partner, device_id_type=MESH)
    pl.semaphore_wait(barrier, len(partners))


class PlaneGather:
    def __init__(self, me, ref, count, send, recv):
        self.me, self.ref, self.count, self.send, self.recv = me, ref, count, send, recv

    def copy(self, i, k, q, slot):
        far = ((0, 2), (0, 4), (2, 4), (4, 2), (0, 1), (2, 1), (4, 1), (6, 1))[i]
        low, size = ((i - 2) * (BLK // 2), BLK // 2) if i in (2, 3) else (0, BLK)
        part = self.ref.at[k, self.count * (self.me ^ far[0]) + q, pl.ds(low, size)]
        return pltpu.make_async_remote_copy(
            src_ref=part,
            dst_ref=part,
            send_sem=self.send.at[i, slot],
            recv_sem=self.recv.at[i, slot],
            device_id={"col": self.me ^ far[1]},
            device_id_type=MESH,
        )

    def begin(self, *at):
        for i in (0, 1, 4):
            self.copy(i, *at).start()

    def relay(self, *at):
        for i in (0, 1):
            self.copy(i, *at).wait_recv()
            self.copy(i + 2, *at).start()
            self.copy(i + 5, *at).start()

    def across(self, *at):
        self.copy(2, *at).wait_recv()
        self.copy(3, *at).wait_recv()
        self.copy(7, *at).start()

    def land(self, *at):
        for i in range(4, 8):
            self.copy(i, *at).wait_recv()

    def settle(self, *at):
        for i in range(8):
            self.copy(i, *at).wait_send()


def row_copy(place, flip, src, dst, send, recv):
    return pltpu.make_async_remote_copy(
        src_ref=src,
        dst_ref=dst,
        send_sem=send,
        recv_sem=recv,
        device_id={"row": place ^ flip},
        device_id_type=MESH,
    )


def f32_sum(*terms):
    total = terms[0].astype(jnp.float32)
    for term in terms[1:]:
        total = total + term.astype(jnp.float32)
    return total


AHEAD = 5
RELAY, ACROSS = 4, 8


def down_kernel(
    chunks, inverse_ref, coupling_ref, rhs_ref, root_ref, low_ref, update_ref, given_ref,
    a_ref, c_ref, acc_ref, w_ref, r_ref, send, recv, a_sem, c_sem, given_send, given_recv,
):
    me = lax.axis_index("col")

    def load(j):
        return pltpu.make_async_copy(
            inverse_ref.at[pl.ds(pl.multiple_of(j * CHUNK, CHUNK), CHUNK)],
            a_ref.at[j],
            a_sem.at[j],
        )

    for j in range(AHEAD):
        load(j).start()
    enter([{"col": me ^ (1 << b)} for b in range(3)])
    mine = root_ref.shape[0] // BLK
    given = PlaneGather(me, given_ref, mine, given_send, given_recv)
    for q in range(mine):
        given_ref[0, mine * me + q] = root_ref[pl.ds(q * BLK, BLK)].astype(jnp.bfloat16)
        given.begin(0, q, q)
    acc_ref[...] = jnp.zeros_like(acc_ref)
    whole = pltpu.make_async_copy(coupling_ref, c_ref, c_sem)

    def produce(j):
        load(j).wait()

        @pl.when(j + AHEAD < chunks)
        def _():
            load(j + AHEAD).start()

        @pl.when(j + AHEAD == chunks)
        def _():
            whole.start()

        return jnp.dot(a_ref[j], rhs_ref[...], preferred_element_type=jnp.float32).astype(
            jnp.bfloat16
        )

    def consume(j):
        @pl.when(j == 0)
        def _():
            whole.wait()

        columns = pl.ds(pl.multiple_of(j * CHUNK, CHUNK), CHUNK)
        acc_ref[...] += jnp.dot(
            c_ref[:, columns], low_ref[j], preferred_element_type=jnp.float32
        )

    def each(act):
        return lambda: [act(0, q, q) for q in range(mine)] and None

    PlaneSum(me, chunks, w_ref, r_ref, low_ref, send, recv).run(
        produce,
        lambda j, place, value: value,
        consume,
        beside=((RELAY, each(given.relay)), (ACROSS, each(given.across))),
    )
    each(given.land)()
    each(given.settle)()
    update_ref[...] = acc_ref[...].astype(jnp.bfloat16)


def down(child_inverse, coupling, own_rhs, root_rhs, cid):
    rows, depth = child_inverse.shape
    chunks = rows // CHUNK
    coupled = coupling.shape[0]
    vmem = pl.BlockSpec(memory_space=pltpu.VMEM)
    anywhere = pl.BlockSpec(memory_space=pl.ANY)
    mine = root_rhs.shape[0] // BLK
    return pl.pallas_call(
        functools.partial(down_kernel, chunks),
        out_shape=(
            jax.ShapeDtypeStruct((chunks, CHUNK, BLK), jnp.bfloat16),
            jax.ShapeDtypeStruct((coupled, BLK), jnp.bfloat16),
            jax.ShapeDtypeStruct((1, 8 * mine, BLK, BLK), jnp.bfloat16),
        ),
        in_specs=[anywhere, anywhere, vmem, vmem],
        out_specs=(vmem, vmem, vmem),
        scratch_shapes=[
            pltpu.VMEM((chunks, CHUNK, depth), jnp.bfloat16),
            pltpu.VMEM((coupled, rows), jnp.bfloat16),
            pltpu.VMEM((coupled, BLK), jnp.float32),
        ]
        + plane_scratch(chunks, False)
        + [pltpu.SemaphoreType.DMA((chunks,)), pltpu.SemaphoreType.DMA]
        + [pltpu.SemaphoreType.DMA((8, mine))] * 2,
        compiler_params=pltpu.CompilerParams(
            collective_id=cid, has_side_effects=True, vmem_limit_bytes=VMEM
        ),
    )(child_inverse, coupling, own_rhs, root_rhs)


PIECE = 256
LINE_LAGS = (0, 2, 4, 6)


def root_kernel(
    map_ref, update_ref, given_ref, upper_ref, rows_ref,
    u_ref, pair_ref, up_ref, x_ref, y_ref, outer_ref, mid_ref, fin_ref, acc_ref,
    w_ref, r_ref, send, recv,
    pair_sem, cross_sem, up_send, up_recv, line_sem, u_sem,
):
    me = lax.axis_index("col")
    place = lax.axis_index("row")
    child = place >> 1
    is_mid = ((place + 1) >> 1) == 1
    is_end = ((place + 1) >> 1) != 1
    blocks = given_ref.shape[1]
    per = update_ref.shape[0]
    depth, width = upper_ref.shape
    loads = depth // CHUNK

    def load(i):
        rows = pl.ds(i * CHUNK, CHUNK)
        return pltpu.make_async_copy(upper_ref.at[rows], u_ref.at[rows], u_sem.at[i])

    for i in range(loads):
        load(i).start()
    enter(
        [{"col": me ^ (1 << b)} for b in range(3)] + [{"row": place ^ 1}, {"row": place ^ 3}]
    )

    def pair(q):
        return row_copy(
            place, 1, update_ref.at[q], pair_ref.at[q], pair_sem.at[0, q], pair_sem.at[1, q]
        )

    def cross(q):
        part = up_ref.at[child, per * me + q]
        return row_copy(place, 3, part, part, cross_sem.at[0, q], cross_sem.at[1, q])

    def onward(q):
        part = up_ref.at[1 - child, per * me + q]
        return row_copy(place, 1, part, part, cross_sem.at[2, q], cross_sem.at[1, q])

    for q in range(per):
        pair(q).start()
    gather = PlaneGather(me, up_ref, per, up_send, up_recv)
    for q in range(per):
        pair(q).wait_recv()
        up_ref[child, per * me + q] = f32_sum(update_ref[q], pair_ref[q]).astype(jnp.bfloat16)
        pl.when(is_mid)(lambda: cross(q).start())
        gather.begin(child, q, q)
    for q in range(per):
        cross(q).wait_recv()
        pl.when(is_mid)(lambda: onward(q).start())
        gather.begin(1 - child, q, per + q)
        gather.relay(child, q, q)
    for q in range(per):
        gather.relay(1 - child, q, per + q)
        gather.across(child, q, q)
    for q in range(per):
        gather.across(1 - child, q, per + q)
    for q in range(per):
        gather.land(child, q, q)
        gather.land(1 - child, q, per + q)

    def put(j, _):
        value = given_ref[0, j].astype(jnp.float32)
        for k in range(2):
            i = map_ref[k, j]
            block = up_ref[k, jnp.maximum(i, 0)].astype(jnp.float32)
            value = value - jnp.where(i >= 0, block, 0.0)
        x_ref[:, pl.ds(pl.multiple_of(j * BLK, BLK), BLK)] = value.T.astype(jnp.bfloat16)
        return 0

    lax.fori_loop(0, blocks, put, 0, unroll=4)

    pieces = width // PIECE
    half = PIECE // 2
    own = pl.ds(pl.multiple_of(child * half, half), half)
    rest = pl.ds(pl.multiple_of((1 - child) * half, half), half)

    def line(i, p):
        if i == 0:
            src, dst, flip = y_ref.at[p], outer_ref.at[p], 1
        elif i == 1:
            src, dst, flip = y_ref.at[p, rest], mid_ref.at[p], 3
        else:
            src = dst = fin_ref.at[p, rest if i == 4 else own]
            flip = 3 if i == 2 else 1
        return row_copy(place, flip, src, dst, line_sem.at[0, i, p], line_sem.at[1, i, p])

    for i in range(loads):
        load(i).wait()
    def tile(t):
        columns = pl.ds(pl.multiple_of(t * CHUNK, CHUNK), CHUNK)
        out = jnp.dot(x_ref[...], u_ref[:, columns], preferred_element_type=jnp.float32)
        out = out.T.astype(jnp.bfloat16)
        for i in range(CHUNK // PIECE):
            y_ref[t * (CHUNK // PIECE) + i] = out[i * PIECE : (i + 1) * PIECE]

            @pl.when(is_end)
            def _():
                line(0, t * (CHUNK // PIECE) + i).start()

    def line_stage(s, p):
        if s == 0:

            @pl.when(is_mid)
            def _():
                line(0, p).wait_recv()
                y_ref[p, rest] = f32_sum(y_ref[p, rest], outer_ref[p, rest]).astype(jnp.bfloat16)
                line(1, p).start()

        elif s == 1:

            @pl.when(is_mid)
            def _():
                line(1, p).wait_recv()
                fin_ref[p, own] = f32_sum(y_ref[p, own], outer_ref[p, own], mid_ref[p]).astype(
                    jnp.bfloat16
                )
                line(2, p).start()
                line(3, p).start()

        elif s == 2:

            @pl.when(is_mid)
            def _():
                line(2, p).wait_recv()
                line(4, p).start()

        else:

            @pl.when(is_end)
            def _():
                line(3, p).wait_recv()
                line(4, p).wait_recv()

    group = CHUNK // PIECE
    groups = width // CHUNK

    def product(j, g):
        rows = pl.ds(pl.multiple_of(j * CHUNK, CHUNK), CHUNK)
        columns = pl.ds(g * CHUNK, CHUNK)
        part = fin_ref[pl.ds(g * group, group)].reshape(CHUNK, BLK)
        return jnp.dot(u_ref[rows, columns], part, preferred_element_type=jnp.float32)

    def add_group(g):
        def body(j, _):
            value = product(j, g)
            acc_ref[j] = value if g == 0 else acc_ref[j] + value
            return 0

        lax.fori_loop(0, loads, body, 0)

    for t in range(groups):
        tile(t)
    for t in range(pieces + LINE_LAGS[-1]):
        for s in range(4):
            if 0 <= t - LINE_LAGS[s] < pieces:
                line_stage(s, t - LINE_LAGS[s])
        done = t - LINE_LAGS[-1] + 1
        if done > 0 and done % group == 0 and done < pieces:
            add_group(done // group - 1)

    PlaneSum(me, loads, w_ref, r_ref, rows_ref, send, recv).run(
        lambda j: (acc_ref[j] + product(j, groups - 1)).astype(jnp.bfloat16),
        lambda j, at, value: value,
        lambda j: None,
    )

    for q in range(per):
        pair(q).wait_send()
        gather.settle(child, q, q)
        gather.settle(1 - child, q, per + q)

    @pl.when(is_mid)
    def _():
        for q in range(per):
            cross(q).wait_send()
            onward(q).wait_send()
        for p in range(pieces):
            for i in range(1, 5):
                line(i, p).wait_send()

    @pl.when(is_end)
    def _():
        for p in range(pieces):
            line(0, p).wait_send()


def root_part(place_idx, update, given, root_upper, cid):
    depth, width = root_upper.shape
    per = update.shape[0] // BLK
    pieces = width // PIECE
    loads = depth // CHUNK
    vmem = pl.BlockSpec(memory_space=pltpu.VMEM)
    dma = pltpu.SemaphoreType.DMA
    low = jnp.bfloat16
    return pl.pallas_call(
        root_kernel,
        out_shape=jax.ShapeDtypeStruct((loads, CHUNK, BLK), low),
        in_specs=[
            pl.BlockSpec(memory_space=pltpu.SMEM), vmem, vmem, pl.BlockSpec(memory_space=pl.ANY),
        ],
        out_specs=vmem,
        scratch_shapes=[
            pltpu.VMEM((depth, width), low),
            pltpu.VMEM((per, BLK, BLK), low),
            pltpu.VMEM((2, 8 * per, BLK, BLK), low),
            pltpu.VMEM((BLK, depth), low),
            pltpu.VMEM((pieces, PIECE, BLK), low),
            pltpu.VMEM((pieces, PIECE, BLK), low),
            pltpu.VMEM((pieces, PIECE // 2, BLK), low),
            pltpu.VMEM((pieces, PIECE, BLK), low),
            pltpu.VMEM((loads, CHUNK, BLK), jnp.float32),
        ]
        + plane_scratch(loads, False)
        + [
            dma((2, per)), dma((3, per)), dma((8, 2 * per)), dma((8, 2 * per)),
            dma((2, 5, pieces)), dma((loads,)),
        ],
        compiler_params=pltpu.CompilerParams(
            collective_id=cid, has_side_effects=True, vmem_limit_bytes=VMEM
        ),
    )(place_idx, update.reshape(per, BLK, BLK), given, root_upper)


def up_kernel(
    pick_ref, rows_ref, low_ref, coupling_ref, inverse_ref, both_ref,
    c_ref, a_ref, picked_ref, foreign_ref, home_ref, chain_ref, p_ref, acc_ref, part_ref, pair_ref,
    o_ref, w_ref, r_ref, send, recv, pick_sem, final_sem, c_sem, a_sem,
):
    me = lax.axis_index("col")
    place = lax.axis_index("row")
    child = place >> 1
    is_mid = ((place + 1) >> 1) == 1
    is_end = ((place + 1) >> 1) != 1
    per = picked_ref.shape[1]
    chunks = low_ref.shape[0]
    finals = part_ref.shape[0]
    size = part_ref.shape[1]

    whole = pltpu.make_async_copy(coupling_ref, c_ref, c_sem)
    whole.start()

    def load(j):
        rows = pl.ds(pl.multiple_of(j * CHUNK, CHUNK), CHUNK)
        return pltpu.make_async_copy(inverse_ref.at[rows], a_ref.at[j], a_sem.at[j])

    for j in range(chunks):
        load(j).start()
    enter(
        [{"col": me ^ (1 << b)} for b in range(3)] + [{"row": place ^ 1}, {"row": place ^ 3}]
    )

    def pick(q, k):
        i = pick_ref[k * per + q]
        block = rows_ref[jnp.maximum(i, 0)].astype(jnp.float32)
        picked_ref[k, q] = jnp.where(i >= 0, block, 0.0).astype(jnp.bfloat16)

    def hop(i, q):
        src, dst, flip = (
            (picked_ref.at[1 - child, q], foreign_ref.at[q], 1),
            (picked_ref.at[child, q], home_ref.at[q], 1),
            (picked_ref.at[1 - child, q], chain_ref.at[q], 3),
            (picked_ref.at[child, q], home_ref.at[q], 1),
        )[i]
        return row_copy(place, flip, src, dst, pick_sem.at[0, i, q], pick_sem.at[1, i if i < 3 else 1, q])

    for q in range(per):
        pick(q, 1 - child)
        pl.when(is_end)(lambda: hop(0, q).start())
    for q in range(per):
        pick(q, child)
        pl.when(is_end)(lambda: hop(1, q).start())

    @pl.when(is_mid)
    def _():
        for q in range(per):
            hop(0, q).wait_recv()
            picked_ref[1 - child, q] = f32_sum(picked_ref[1 - child, q], foreign_ref[q]).astype(
                jnp.bfloat16
            )
            hop(2, q).start()
        for q in range(per):
            hop(2, q).wait_recv()
            picked_ref[child, q] = f32_sum(picked_ref[child, q], chain_ref[q]).astype(jnp.bfloat16)
            hop(3, q).start()

    for q in range(per):
        hop(1, q).wait_recv()
        p_ref[:, q * BLK : (q + 1) * BLK] = f32_sum(picked_ref[child, q], home_ref[q]).T.astype(
            jnp.bfloat16
        )
    whole.wait()

    def produce(j):
        columns = pl.ds(pl.multiple_of(j * CHUNK, CHUNK), CHUNK)
        out = jnp.dot(p_ref[...], c_ref[:, columns], preferred_element_type=jnp.float32)
        return out.T.astype(jnp.bfloat16)

    def own(j, at, value):
        return low_ref[j, at].astype(jnp.float32) - value

    def consume(j):
        load(j).wait()
        value = jnp.dot(o_ref[j].T, a_ref[j], preferred_element_type=jnp.float32)

        @pl.when(j == 0)
        def _():
            acc_ref[...] = value

        @pl.when(j > 0)
        def _():
            acc_ref[...] += value

    PlaneSum(me, chunks, w_ref, r_ref, o_ref, send, recv).run(produce, own, consume, UP_LAGS)

    def final(i, p):
        if i == 0:
            return row_copy(
                place, 1, part_ref.at[p], pair_ref.at[p], final_sem.at[0, p], final_sem.at[1, p]
            )
        at = both_ref.at[child if i == 1 else 1 - child, p]
        return row_copy(
            place, 3 if i == 1 else 1, at, at, final_sem.at[1 + i, p], final_sem.at[4, p]
        )

    for p in range(finals):
        part_ref[p] = acc_ref[:, p * size : (p + 1) * size].T.astype(jnp.bfloat16)
        final(0, p).start()

    def relay(p):
        final(1, p).wait_recv()
        pl.when(is_mid)(lambda: final(2, p).start())

    for p in range(finals):
        final(0, p).wait_recv()
        both_ref[child, p] = f32_sum(part_ref[p], pair_ref[p]).astype(jnp.bfloat16)
        pl.when(is_mid)(lambda: final(1, p).start())
        if p >= 2:
            pl.when(is_mid)(functools.partial(relay, p - 2))
    for p in range(finals):
        if p < finals - 2:
            pl.when(is_end)(functools.partial(relay, p))
        else:
            relay(p)
    for p in range(finals):
        final(0, p).wait_send()

    @pl.when(is_mid)
    def _():
        for p in range(finals):
            final(1, p).wait_send()
            final(2, p).wait_send()
        for q in range(per):
            hop(2, q).wait_send()
            hop(3, q).wait_send()

    @pl.when(is_end)
    def _():
        for q in range(per):
            hop(0, q).wait_send()
            hop(1, q).wait_send()


UP_LAGS = FAR


def up_part(pick_idx, rows_low, child_low, coupling, child_inverse, cid):
    rows, width = child_inverse.shape
    coupled = coupling.shape[0]
    per = coupled // BLK
    chunks = rows // CHUNK
    finals = width // 256
    vmem = pl.BlockSpec(memory_space=pltpu.VMEM)
    anywhere = pl.BlockSpec(memory_space=pl.ANY)
    dma = pltpu.SemaphoreType.DMA
    low = jnp.bfloat16
    return pl.pallas_call(
        up_kernel,
        out_shape=jax.ShapeDtypeStruct((2, finals, width // finals, BLK), low),
        in_specs=[pl.BlockSpec(memory_space=pltpu.SMEM), vmem, vmem, anywhere, anywhere],
        out_specs=vmem,
        scratch_shapes=[
            pltpu.VMEM((coupled, rows), low),
            pltpu.VMEM((chunks, CHUNK, width), low),
            pltpu.VMEM((2, per, BLK, BLK), low),
            pltpu.VMEM((per, BLK, BLK), low),
            pltpu.VMEM((per, BLK, BLK), low),
            pltpu.VMEM((per, BLK, BLK), low),
            pltpu.VMEM((BLK, coupled), low),
            pltpu.VMEM((BLK, width), jnp.float32),
            pltpu.VMEM((finals, width // finals, BLK), low),
            pltpu.VMEM((finals, width // finals, BLK), low),
            pltpu.VMEM((chunks, CHUNK, BLK), low),
        ]
        + plane_scratch(chunks, False)
        + [dma((2, 4, per)), dma((5, finals)), dma, dma((chunks,))],
        compiler_params=pltpu.CompilerParams(
            collective_id=cid, has_side_effects=True, vmem_limit_bytes=VMEM
        ),
    )(pick_idx, rows_low, child_low, coupling, child_inverse)


def finish_kernel(x_ref, rows_ref, o_ref, root_ref, own_ref, sem):
    own = own_ref.shape[0]
    copy = pltpu.make_async_copy(
        rows_ref.at[pl.ds(pl.multiple_of(lax.axis_index("col") * own, own), own)], own_ref, sem
    )
    copy.start()
    step = 64

    def body(i, _):
        rows = pl.ds(pl.multiple_of(i * step, step), step)
        for k in range(2):
            o_ref[rows, k, :] = x_ref[k, rows, :].astype(jnp.float32)
        return 0

    lax.fori_loop(0, o_ref.shape[0] // step, body, 0, unroll=4)
    copy.wait()
    root_ref[...] = own_ref[...].astype(jnp.float32)


def local(row_devices, col_devices, child_inverse, root_upper, coupling, child_rhs, root_rhs, child_map):
    row_place = lax.axis_index("row")
    col_place = lax.axis_index("col")
    child_slot = row_place // (row_devices // 2)
    root_rows = root_upper.shape[0]
    coupled = coupling.shape[0]
    rhs_width = child_rhs.shape[2]
    vmem = pl.BlockSpec(memory_space=pltpu.VMEM)
    smem = pl.BlockSpec(memory_space=pltpu.SMEM)
    row_bits = list(range(bits_of(row_devices)))
    col_bits = list(range(bits_of(col_devices)))
    col_orders = [col_bits, col_bits[:1] + col_bits[:0:-1]] * 2
    row_orders = [row_bits, row_bits[::-1]] * 2
    pick_order = [row_bits[-1:] + row_bits[:-1]]
    contract_first = (((0,), (0,)), ((), ()))

    per_col = coupled // BLK
    root_blocks = root_rows // BLK
    local_map = lax.dynamic_slice_in_dim(child_map, col_place * per_col, per_col, 1)
    target = local_map - row_place * root_blocks
    block_hits = target[:, :, None] == jnp.arange(root_blocks, dtype=jnp.int32)[None, None, :]
    slots = jnp.arange(2 * per_col, dtype=jnp.int32).reshape(2, per_col, 1)
    place_idx = jnp.max(jnp.where(block_hits, slots, -1), axis=1)
    pick_idx = jnp.where((target >= 0) & (target < root_blocks), target, -1).reshape(-1)
    rhs_rows = root_rhs.shape[0]
    given_rows = lax.dynamic_update_slice(
        jnp.zeros((root_rows, rhs_width), jnp.float32),
        root_rhs,
        (col_place * rhs_rows, jnp.int32(0)),
    )

    own_rhs = lax.dynamic_index_in_dim(child_rhs, child_slot, 1, keepdims=False).astype(
        jnp.bfloat16
    )
    child_low = all_sum(
        jnp.dot(child_inverse, own_rhs, preferred_element_type=jnp.float32).astype(jnp.bfloat16),
        "col", col_devices, col_orders, 0,
    )
    update = jnp.dot(coupling, child_low, preferred_element_type=jnp.float32)
    update_both = both_sum(update.astype(jnp.bfloat16), "row", row_devices, 2, 1)
    root_term = pl.pallas_call(
        place_kernel,
        out_shape=jax.ShapeDtypeStruct((root_blocks, BLK, rhs_width), jnp.bfloat16),
        in_specs=[smem, vmem, vmem],
        out_specs=vmem,
    )(
        place_idx,
        update_both.reshape(2 * per_col, BLK, rhs_width),
        given_rows.reshape(root_blocks, BLK, rhs_width),
    )
    root_low = all_sum(
        root_term.reshape(root_rows, rhs_width), "col", col_devices, col_orders, 2
    )
    solved_low = all_sum(
        lax.dot_general(
            root_upper, root_low, contract_first, preferred_element_type=jnp.float32
        ).astype(jnp.bfloat16),
        "row", row_devices, row_orders, 3,
    )
    rows_low = all_sum(
        jnp.dot(root_upper, solved_low, preferred_element_type=jnp.float32).astype(jnp.bfloat16),
        "col", col_devices, col_orders, 4,
    )
    root_solution = lax.dynamic_slice_in_dim(rows_low, col_place * rhs_rows, rhs_rows, 0).astype(
        jnp.float32
    )
    picked = pl.pallas_call(
        pick_kernel,
        out_shape=jax.ShapeDtypeStruct((2 * per_col, BLK, rhs_width), jnp.bfloat16),
        in_specs=[smem, vmem],
        out_specs=vmem,
    )(pick_idx, rows_low.reshape(root_blocks, BLK, rhs_width))
    picked_half = all_sum(
        picked.reshape(2 * coupled, rhs_width), "row", row_devices, pick_order, 5,
        gathers=len(row_bits) - 1,
    )
    own_pick = lax.dynamic_slice_in_dim(picked_half, child_slot * coupled, coupled, 0)
    back_term = all_sum(
        lax.dot_general(
            coupling, own_pick, contract_first, preferred_element_type=jnp.float32
        ).astype(jnp.bfloat16),
        "col", col_devices, col_orders, 6,
    )
    adjusted = (child_low.astype(jnp.float32) - back_term.astype(jnp.float32)).astype(
        jnp.bfloat16
    )
    final_rows = lax.dot_general(
        child_inverse, adjusted, contract_first, preferred_element_type=jnp.float32
    )
    final_both = both_sum(final_rows.astype(jnp.bfloat16), "row", row_devices, 4, 7)
    child_solution = pl.pallas_call(
        weave_kernel,
        out_shape=jax.ShapeDtypeStruct(child_rhs.shape, jnp.float32),
        in_specs=[vmem],
        out_specs=vmem,
    )(final_both)
    return (root_solution, child_solution)


def near(row_devices, col_devices, child_inverse, root_upper, coupling, child_rhs, root_rhs, child_map):
    row_place = lax.axis_index("row")
    col_place = lax.axis_index("col")
    child_slot = row_place // (row_devices // 2)
    root_rows = root_upper.shape[0]
    coupled = coupling.shape[0]
    rhs_width = child_rhs.shape[2]
    vmem = pl.BlockSpec(memory_space=pltpu.VMEM)

    per_col = coupled // BLK
    root_blocks = root_rows // BLK
    local_map = lax.dynamic_slice_in_dim(child_map, col_place * per_col, per_col, 1)
    target = local_map - row_place * root_blocks
    block_hits = (child_map - row_place * root_blocks)[:, :, None] == jnp.arange(root_blocks, dtype=jnp.int32)[None, None, :]
    slots = jnp.arange(child_map.shape[1], dtype=jnp.int32).reshape(1, -1, 1)
    place_idx = jnp.max(jnp.where(block_hits, slots, -1), axis=1)
    pick_idx = jnp.where((target >= 0) & (target < root_blocks), target, -1).reshape(-1)

    own_rhs = lax.dynamic_index_in_dim(child_rhs, child_slot, 1, keepdims=False).astype(
        jnp.bfloat16
    )
    child_low, update, given = down(child_inverse, coupling, own_rhs, root_rhs, 0)
    rows_low = root_part(place_idx, update, given, root_upper, 1)
    both = up_part(
        pick_idx, rows_low.reshape(root_blocks, BLK, rhs_width), child_low, coupling,
        child_inverse, 2,
    )
    anywhere = pl.BlockSpec(memory_space=pl.ANY)
    child_solution, root_solution = pl.pallas_call(
        finish_kernel,
        out_shape=(
            jax.ShapeDtypeStruct(child_rhs.shape, jnp.float32),
            jax.ShapeDtypeStruct(root_rhs.shape, jnp.float32),
        ),
        in_specs=[vmem, anywhere],
        out_specs=(vmem, vmem),
        scratch_shapes=[
            pltpu.VMEM(root_rhs.shape, jnp.bfloat16), pltpu.SemaphoreType.DMA,
        ],
    )(both.reshape(2, -1, rhs_width), rows_low.reshape(-1, rhs_width))
    return (root_solution, child_solution)


def solution(mesh):
    body = near if (mesh.shape["row"], mesh.shape["col"]) == (4, 8) else local
    return jax.shard_map(
        functools.partial(body, mesh.shape["row"], mesh.shape["col"]),
        mesh=mesh,
        in_specs=(
            P("row", "col"),
            P("row", "col"),
            P("col", "row"),
            P("col", None, None),
            P(("row", "col"), None),
            P(),
        ),
        out_specs=(P(("row", "col"), None), P("col", None, None)),
        check_vma=False,
    )
```

```python
import functools

import jax
import jax.numpy as jnp
from jax import lax
from jax.experimental import pallas as pl
from jax.experimental.pallas import tpu as pltpu
from jax.sharding import PartitionSpec as P

BLK = 128
MESH = pl.DeviceIdType.MESH
VMEM = 58 * 2**20


def bits_of(n):
    m = n.bit_length() - 1
    assert 1 << m == n
    return m


def greet(axis, me, bits):
    barrier = pltpu.get_barrier_semaphore()
    for b in bits:
        pl.semaphore_signal(
            barrier, inc=1, device_id={axis: me ^ (1 << b)}, device_id_type=MESH
        )
    pl.semaphore_wait(barrier, len(bits))


def remote(axis, me, bit, src, dst, send, recv):
    copy = pltpu.make_async_remote_copy(
        src_ref=src,
        dst_ref=dst,
        send_sem=send,
        recv_sem=recv,
        device_id={axis: me ^ (1 << bit)},
        device_id_type=MESH,
    )
    copy.start()
    return copy


def run_streams(streams, steps, begin, finish):
    copies = [[begin(s, 0)] for s in range(streams)]
    for t in range(steps):
        for s in range(streams):
            copies[s][t].wait_recv()
            finish(s, t)
            if t + 1 < steps:
                copies[s].append(begin(s, t + 1))
    for own in copies:
        for copy in own:
            copy.wait_send()


def spans(me, order, n):
    low = jnp.int32(0)
    size = n
    offset = 0
    out = []
    for b in order:
        half = size // 2
        mine = (me >> b) & 1
        keep, away = low + mine * half, low + (1 - mine) * half
        out.append((keep, away, half, offset))
        low, size, offset = keep, half, offset + half
    return out


def add_landed(s, span, src, r_ref, put):
    keep, _, half, offset = span

    def add(i, _):
        total = src[s, keep + i].astype(jnp.float32) + r_ref[s, offset + i].astype(jnp.float32)
        put(keep + i, total.astype(jnp.bfloat16))
        return 0

    lax.fori_loop(0, half, add, 0)


def all_sum_kernel(axis, n, orders, gathers, x_ref, o_ref, w_ref, r_ref, send, recv):
    me = lax.axis_index(axis)
    steps = len(orders[0])
    plans = [spans(me, order, n) for order in orders]
    greet(axis, me, list(range(steps)))

    def begin(s, t):
        if t < steps:
            _, away, half, offset = plans[s][t]
            src = (x_ref if t == 0 else w_ref).at[s, pl.ds(away, half)]
            dst = r_ref.at[s, pl.ds(offset, half)]
            bit = orders[s][t]
        else:
            back = 2 * steps - 1 - t
            src = dst = o_ref.at[s, pl.ds(plans[s][back][0], plans[s][back][2])]
            bit = orders[s][back]
        return remote(axis, me, bit, src, dst, send.at[s, t], recv.at[s, t])

    def finish(s, t):
        if t < steps:

            def put(place, value):
                if t == steps - 1:
                    o_ref[s, place] = value
                else:
                    w_ref[s, place] = value

            add_landed(s, plans[s][t], x_ref if t == 0 else w_ref, r_ref, put)

    run_streams(len(orders), steps + gathers, begin, finish)


def all_sum(x, axis, n, orders, cid, gathers=None):
    rows, width = x.shape
    m = bits_of(n)
    gathers = m if gathers is None else gathers
    streams = len(orders)
    shape = (streams, n, rows // (streams * n), width)
    out = pl.pallas_call(
        functools.partial(all_sum_kernel, axis, n, orders, gathers),
        out_shape=jax.ShapeDtypeStruct(shape, jnp.bfloat16),
        in_specs=[pl.BlockSpec(memory_space=pltpu.VMEM)],
        out_specs=pl.BlockSpec(memory_space=pltpu.VMEM),
        scratch_shapes=[
            pltpu.VMEM(shape, jnp.bfloat16),
            pltpu.VMEM(shape, jnp.bfloat16),
            pltpu.SemaphoreType.DMA((streams, 2 * m)),
            pltpu.SemaphoreType.DMA((streams, 2 * m)),
        ],
        compiler_params=pltpu.CompilerParams(collective_id=cid, has_side_effects=True),
    )(x.reshape(shape))
    return out.reshape(rows, width)


def both_sum_kernel(axis, n, streams, x_ref, o_ref, w_ref, r_ref, send, recv):
    me = lax.axis_index(axis)
    m = bits_of(n)
    slot = me >> (m - 1)
    plan = spans(me, list(range(m - 1)), n // 2)
    greet(axis, me, list(range(m)))

    def begin(s, t):
        if t < m - 1:
            _, away, half, offset = plan[t]
            src = (x_ref if t == 0 else w_ref).at[s, pl.ds(away, half)]
            dst = r_ref.at[s, pl.ds(offset, half)]
            bit = t
        elif t == m - 1:
            src = dst = o_ref.at[slot, s, pl.ds(plan[-1][0], 1)]
            bit = m - 1
        else:
            bit = 2 * (m - 1) - t
            src = dst = o_ref.at[:, s, pl.ds(plan[bit][0], plan[bit][2])]
        return remote(axis, me, bit, src, dst, send.at[s, t], recv.at[s, t])

    def finish(s, t):
        if t < m - 1:

            def put(place, value):
                if t == m - 2:
                    o_ref[slot, s, place] = value
                else:
                    w_ref[s, place] = value

            add_landed(s, plan[t], x_ref if t == 0 else w_ref, r_ref, put)

    run_streams(streams, 2 * m - 1, begin, finish)


def both_sum(x, axis, n, streams, cid):
    rows, width = x.shape
    m = bits_of(n)
    half = n // 2
    shape = (streams, half, rows // (streams * half), width)
    out = pl.pallas_call(
        functools.partial(both_sum_kernel, axis, n, streams),
        out_shape=jax.ShapeDtypeStruct((2,) + shape, jnp.bfloat16),
        in_specs=[pl.BlockSpec(memory_space=pltpu.VMEM)],
        out_specs=pl.BlockSpec(memory_space=pltpu.VMEM),
        scratch_shapes=[
            pltpu.VMEM(shape, jnp.bfloat16),
            pltpu.VMEM(shape, jnp.bfloat16),
            pltpu.SemaphoreType.DMA((streams, 2 * m)),
            pltpu.SemaphoreType.DMA((streams, 2 * m)),
        ],
        compiler_params=pltpu.CompilerParams(collective_id=cid, has_side_effects=True),
    )(x.reshape(shape))
    return out.reshape(2, rows, width)


def place_kernel(idx_ref, update_ref, given_ref, o_ref):
    def body(j, _):
        value = given_ref[j]
        for k in range(2):
            i = idx_ref[k, j]
            block = update_ref[jnp.maximum(i, 0)].astype(jnp.float32)
            value = value - jnp.where(i >= 0, block, 0.0)
        o_ref[j] = value.astype(jnp.bfloat16)
        return 0

    lax.fori_loop(0, o_ref.shape[0], body, 0)


def pick_kernel(idx_ref, rows_ref, o_ref):
    def body(j, _):
        i = idx_ref[j]
        block = rows_ref[jnp.maximum(i, 0)].astype(jnp.float32)
        o_ref[j] = jnp.where(i >= 0, block, 0.0).astype(jnp.bfloat16)
        return 0

    lax.fori_loop(0, o_ref.shape[0], body, 0)


def weave_kernel(x_ref, o_ref):
    step = 64

    def body(i, _):
        rows = pl.ds(pl.multiple_of(i * step, step), step)
        for k in range(2):
            o_ref[rows, k, :] = x_ref[k, rows, :].astype(jnp.float32)
        return 0

    lax.fori_loop(0, o_ref.shape[0] // step, body, 0)


CHUNK = 512
FAR = (0, 2, 6, 10, 14, 18, 20)


class PlaneSum:
    def __init__(self, me, chunks, w_ref, r_ref, o_ref, send, recv):
        self.me, self.chunks = me, chunks
        self.w, self.r, self.o = w_ref, r_ref, o_ref
        self.send, self.recv = send, recv

    def bits(self, j):
        first = 1 + j % 2
        return 0, first, 3 - first

    def keeps(self, j):
        low, size, out = 0, CHUNK, []
        for b in self.bits(j):
            size = size // 2
            mine = (self.me >> b) & 1
            out.append((low + mine * size, low + (1 - mine) * size, size))
            low = low + mine * size
        return out

    def copy(self, s, j):
        bits, keeps = self.bits(j), self.keeps(j)
        if s < 3:
            _, away, size = keeps[s]
            src = self.w.at[j, pl.ds(pl.multiple_of(away, size), size)]
            dst = self.r.at[j, pl.ds(CHUNK - 2 * size, size)]
            bit = bits[s]
        else:
            keep, _, size = keeps[5 - s]
            src = dst = self.o.at[j, pl.ds(pl.multiple_of(keep, size), size)]
            bit = bits[5 - s]
        return pltpu.make_async_remote_copy(
            src_ref=src,
            dst_ref=dst,
            send_sem=self.send.at[s, j],
            recv_sem=self.recv.at[s, j],
            device_id={"col": self.me ^ (1 << bit)},
            device_id_type=MESH,
        )

    def total(self, s, j, low, size):
        keep, _, half = self.keeps(j)[s]
        mine = self.w[j, pl.ds(pl.multiple_of(keep + low, size), size)].astype(jnp.float32)
        landed = self.r[j, pl.ds(pl.multiple_of(CHUNK - 2 * half + low, size), size)]
        return mine + landed.astype(jnp.float32)

    def fold(self, s, j):
        self.copy(s, j).wait_recv()
        keep, _, half = self.keeps(j)[s]
        size = half // 2
        stay = ((self.me >> self.bits(j)[s + 1]) & 1) * size
        for low, last in ((size - stay, False), (stay, True)):
            self.w[j, pl.ds(pl.multiple_of(keep + low, size), size)] = self.total(
                s, j, low, size
            ).astype(jnp.bfloat16)
            if not last:
                self.copy(s + 1, j).start()

    def run(self, produce, own, consume, lags=FAR, beside=()):
        def stage(k, j):
            if k == 0:
                self.w[j] = produce(j)
                self.copy(0, j).start()
            elif k < 3:
                self.fold(k - 1, j)
            elif k == 3:
                self.copy(2, j).wait_recv()
                keep, _, size = self.keeps(j)[2]
                place = pl.ds(pl.multiple_of(keep, size), size)
                self.o[j, place] = own(j, place, self.total(2, j, 0, size)).astype(jnp.bfloat16)
                self.copy(3, j).start()
            else:
                self.copy(k - 1, j).wait_recv()
                if k < 6:
                    self.copy(k, j).start()
                else:
                    consume(j)

        def tick(t, _):
            for k in reversed(range(7)):
                j = t - lags[k]
                pl.when((j >= 0) & (j < self.chunks))(functools.partial(stage, k, j))
            for at, act in beside:
                pl.when(t == at)(act)
            return 0

        lax.fori_loop(0, self.chunks + lags[-1], tick, 0)

        def settle(j, _):
            for s in range(6):
                self.copy(s, j).wait_send()
            return 0

        lax.fori_loop(0, self.chunks, settle, 0)


def plane_scratch(chunks, with_out):
    out = [
        pltpu.VMEM((chunks, CHUNK, BLK), jnp.bfloat16),
        pltpu.VMEM((chunks, CHUNK, BLK), jnp.bfloat16),
    ]
    if with_out:
        out.append(pltpu.VMEM((chunks, CHUNK, BLK), jnp.bfloat16))
    return out + [pltpu.SemaphoreType.DMA((6, chunks)), pltpu.SemaphoreType.DMA((6, chunks))]


def enter(partners):
    barrier = pltpu.get_barrier_semaphore()
    for partner in partners:
        pl.semaphore_signal(barrier, inc=1, device_id=partner, device_id_type=MESH)
    pl.semaphore_wait(barrier, len(partners))


class PlaneGather:
    def __init__(self, me, ref, count, send, recv):
        self.me, self.ref, self.count, self.send, self.recv = me, ref, count, send, recv

    def copy(self, i, k, q, slot, direct=False):
        far = ((0, 2), (0, 4), (2, 4), (4, 2), (0, 1), (2, 1), (4, 1), (6, 1))[i]
        low, size = ((i - 2) * (BLK // 2), BLK // 2) if i in (2, 3) else (0, BLK)
        if direct and i == 2:
            far, size = (0, 6), BLK
        part = self.ref.at[k, self.count * (self.me ^ far[0]) + q, pl.ds(low, size)]
        return pltpu.make_async_remote_copy(
            src_ref=part,
            dst_ref=part,
            send_sem=self.send.at[i, slot],
            recv_sem=self.recv.at[i, slot],
            device_id={"col": self.me ^ far[1]},
            device_id_type=MESH,
        )

    def begin(self, k, q, slot, direct=False):
        for i in (0, 1, 2, 4) if direct else (0, 1, 4):
            self.copy(i, k, q, slot, direct).start()

    def relay(self, k, q, slot, direct=False):
        for i in (0, 1):
            self.copy(i, k, q, slot).wait_recv()
            if not direct:
                self.copy(i + 2, k, q, slot).start()
            self.copy(i + 5, k, q, slot).start()

    def across(self, k, q, slot, direct=False):
        self.copy(2, k, q, slot, direct).wait_recv()
        if not direct:
            self.copy(3, k, q, slot).wait_recv()
        self.copy(7, k, q, slot).start()

    def land(self, *at):
        for i in range(4, 8):
            self.copy(i, *at).wait_recv()

    def settle(self, k, q, slot, direct=False):
        for i in range(8):
            if not (direct and i == 3):
                self.copy(i, k, q, slot, direct).wait_send()


def row_copy(place, flip, src, dst, send, recv):
    return pltpu.make_async_remote_copy(
        src_ref=src,
        dst_ref=dst,
        send_sem=send,
        recv_sem=recv,
        device_id={"row": place ^ flip},
        device_id_type=MESH,
    )


def f32_sum(*terms):
    total = terms[0].astype(jnp.float32)
    for term in terms[1:]:
        total = total + term.astype(jnp.float32)
    return total


AHEAD = 5
RELAY, ACROSS = 4, 8


def down_kernel(
    chunks, inverse_ref, coupling_ref, rhs_ref, root_ref, low_ref, update_ref, given_ref,
    a_ref, c_ref, acc_ref, w_ref, r_ref, send, recv, a_sem, c_sem, given_send, given_recv,
):
    me = lax.axis_index("col")

    def load(j):
        return pltpu.make_async_copy(
            inverse_ref.at[pl.ds(pl.multiple_of(j * CHUNK, CHUNK), CHUNK)],
            a_ref.at[j],
            a_sem.at[j],
        )

    for j in range(AHEAD):
        load(j).start()
    enter([{"col": me ^ (1 << b)} for b in range(3)])
    mine = root_ref.shape[0] // BLK
    given = PlaneGather(me, given_ref, mine, given_send, given_recv)
    for q in range(mine):
        given_ref[0, mine * me + q] = root_ref[pl.ds(q * BLK, BLK)].astype(jnp.bfloat16)
        given.begin(0, q, q)
    acc_ref[...] = jnp.zeros_like(acc_ref)
    whole = pltpu.make_async_copy(coupling_ref, c_ref, c_sem)

    def produce(j):
        load(j).wait()

        @pl.when(j + AHEAD < chunks)
        def _():
            load(j + AHEAD).start()

        @pl.when(j + AHEAD == chunks)
        def _():
            whole.start()

        return jnp.dot(a_ref[j], rhs_ref[...], preferred_element_type=jnp.float32).astype(
            jnp.bfloat16
        )

    def consume(j):
        @pl.when(j == 0)
        def _():
            whole.wait()

        columns = pl.ds(pl.multiple_of(j * CHUNK, CHUNK), CHUNK)
        acc_ref[...] += jnp.dot(
            c_ref[:, columns], low_ref[j], preferred_element_type=jnp.float32
        )

    def each(act):
        return lambda: [act(0, q, q) for q in range(mine)] and None

    PlaneSum(me, chunks, w_ref, r_ref, low_ref, send, recv).run(
        produce,
        lambda j, place, value: value,
        consume,
        beside=((RELAY, each(given.relay)), (ACROSS, each(given.across))),
    )
    each(given.land)()
    each(given.settle)()
    update_ref[...] = acc_ref[...].astype(jnp.bfloat16)


def down(child_inverse, coupling, own_rhs, root_rhs, cid):
    rows, depth = child_inverse.shape
    chunks = rows // CHUNK
    coupled = coupling.shape[0]
    vmem = pl.BlockSpec(memory_space=pltpu.VMEM)
    anywhere = pl.BlockSpec(memory_space=pl.ANY)
    mine = root_rhs.shape[0] // BLK
    return pl.pallas_call(
        functools.partial(down_kernel, chunks),
        out_shape=(
            jax.ShapeDtypeStruct((chunks, CHUNK, BLK), jnp.bfloat16),
            jax.ShapeDtypeStruct((coupled, BLK), jnp.bfloat16),
            jax.ShapeDtypeStruct((1, 8 * mine, BLK, BLK), jnp.bfloat16),
        ),
        in_specs=[anywhere, anywhere, vmem, vmem],
        out_specs=(vmem, vmem, vmem),
        scratch_shapes=[
            pltpu.VMEM((chunks, CHUNK, depth), jnp.bfloat16),
            pltpu.VMEM((coupled, rows), jnp.bfloat16),
            pltpu.VMEM((coupled, BLK), jnp.float32),
        ]
        + plane_scratch(chunks, False)
        + [pltpu.SemaphoreType.DMA((chunks,)), pltpu.SemaphoreType.DMA]
        + [pltpu.SemaphoreType.DMA((8, mine))] * 2,
        compiler_params=pltpu.CompilerParams(
            collective_id=cid, has_side_effects=True, vmem_limit_bytes=VMEM
        ),
    )(child_inverse, coupling, own_rhs, root_rhs)


PIECE = 256
LINE_LAGS = (0, 2, 4)
ROOT_LAGS = (0, 4, 11, 17, 23, 29, 33)


def root_kernel(
    map_ref, update_ref, given_ref, upper_ref, rows_ref,
    u_ref, pair_ref, up_ref, x_ref, y_ref, outer_ref, mid_ref, inward_ref, outward_ref, fin_ref,
    acc_ref,
    w_ref, r_ref, send, recv,
    pair_sem, cross_sem, up_send, up_recv, line_sem, u_sem,
):
    me = lax.axis_index("col")
    place = lax.axis_index("row")
    child = place >> 1
    is_mid = ((place + 1) >> 1) == 1
    is_end = ((place + 1) >> 1) != 1
    blocks = given_ref.shape[1]
    per = update_ref.shape[0]
    depth, width = upper_ref.shape
    loads = depth // CHUNK

    def load(i):
        rows = pl.ds(i * CHUNK, CHUNK)
        return pltpu.make_async_copy(upper_ref.at[rows], u_ref.at[rows], u_sem.at[i])

    for i in range(loads):
        load(i).start()
    enter(
        [{"col": me ^ b} for b in (1, 2, 4, 6)] + [{"row": place ^ 1}, {"row": place ^ 3}]
    )

    def pair(q):
        return row_copy(
            place, 1, update_ref.at[q], pair_ref.at[q], pair_sem.at[0, q], pair_sem.at[1, q]
        )

    def cross(q):
        part = up_ref.at[child, per * me + q]
        return row_copy(place, 3, part, part, cross_sem.at[0, q], cross_sem.at[1, q])

    def onward(q):
        part = up_ref.at[1 - child, per * me + q]
        return row_copy(place, 1, part, part, cross_sem.at[2, q], cross_sem.at[1, q])

    for q in range(per):
        pair(q).start()
    gather = PlaneGather(me, up_ref, per, up_send, up_recv)
    for q in range(per):
        pair(q).wait_recv()
        up_ref[child, per * me + q] = f32_sum(update_ref[q], pair_ref[q]).astype(jnp.bfloat16)
        pl.when(is_mid)(lambda: cross(q).start())
        gather.begin(child, q, q)
    for q in range(per):
        cross(q).wait_recv()
        pl.when(is_mid)(lambda: onward(q).start())
        gather.begin(1 - child, q, per + q, True)
        gather.relay(child, q, q)
    for q in range(per):
        gather.across(child, q, q)
    for q in range(per):
        gather.relay(1 - child, q, per + q, True)
        gather.across(1 - child, q, per + q, True)
    for q in range(per):
        gather.land(child, q, q)
        gather.land(1 - child, q, per + q)

    def put(j, _):
        value = given_ref[0, j].astype(jnp.float32)
        for k in range(2):
            i = map_ref[k, j]
            block = up_ref[k, jnp.maximum(i, 0)].astype(jnp.float32)
            value = value - jnp.where(i >= 0, block, 0.0)
        x_ref[:, pl.ds(pl.multiple_of(j * BLK, BLK), BLK)] = value.T.astype(jnp.bfloat16)
        return 0

    lax.fori_loop(0, blocks, put, 0, unroll=4)

    pieces = width // PIECE

    def line(i, p):
        src, dst, flip = (
            (y_ref.at[p], outer_ref.at[p], 1),
            (inward_ref.at[p], mid_ref.at[p], 3),
            (outward_ref.at[p], outer_ref.at[p], 1),
        )[i]
        return row_copy(place, flip, src, dst, line_sem.at[0, i, p], line_sem.at[1, i % 2, p])

    for i in range(loads):
        load(i).wait()
    def tile(t):
        columns = pl.ds(pl.multiple_of(t * CHUNK, CHUNK), CHUNK)
        out = jnp.dot(x_ref[...], u_ref[:, columns], preferred_element_type=jnp.float32)
        out = out.T.astype(jnp.bfloat16)
        for i in range(CHUNK // PIECE):
            y_ref[t * (CHUNK // PIECE) + i] = out[i * PIECE : (i + 1) * PIECE]

            @pl.when(is_end)
            def _():
                line(0, t * (CHUNK // PIECE) + i).start()

    def line_stage(s, p):
        if s == 0:

            @pl.when(is_mid)
            def _():
                line(0, p).wait_recv()
                inward_ref[p] = f32_sum(y_ref[p], outer_ref[p]).astype(jnp.bfloat16)
                line(1, p).start()

        elif s == 1:

            @pl.when(is_mid)
            def _():
                line(1, p).wait_recv()
                both = f32_sum(y_ref[p], mid_ref[p])
                outward_ref[p] = both.astype(jnp.bfloat16)
                line(2, p).start()
                fin_ref[p] = (both + outer_ref[p].astype(jnp.float32)).astype(jnp.bfloat16)

        else:

            @pl.when(is_end)
            def _():
                line(2, p).wait_recv()
                fin_ref[p] = f32_sum(y_ref[p], outer_ref[p]).astype(jnp.bfloat16)

    group = CHUNK // PIECE
    groups = width // CHUNK

    def product(j, g):
        rows = pl.ds(pl.multiple_of(j * CHUNK, CHUNK), CHUNK)
        columns = pl.ds(g * CHUNK, CHUNK)
        part = fin_ref[pl.ds(g * group, group)].reshape(CHUNK, BLK)
        return jnp.dot(u_ref[rows, columns], part, preferred_element_type=jnp.float32)

    def add_group(g):
        def body(j, _):
            value = product(j, g)
            acc_ref[j] = value if g == 0 else acc_ref[j] + value
            return 0

        lax.fori_loop(0, loads, body, 0)

    for t in range(groups):
        tile(t)
    for t in range(pieces + LINE_LAGS[-1]):
        for s in range(3):
            if 0 <= t - LINE_LAGS[s] < pieces:
                line_stage(s, t - LINE_LAGS[s])
        done = t - LINE_LAGS[-1] + 1
        if done > 0 and done % group == 0 and done < pieces:
            add_group(done // group - 1)

    PlaneSum(me, loads, w_ref, r_ref, rows_ref, send, recv).run(
        lambda j: (acc_ref[j] + product(j, groups - 1)).astype(jnp.bfloat16),
        lambda j, at, value: value,
        lambda j: None,
        ROOT_LAGS,
    )

    for q in range(per):
        pair(q).wait_send()
        gather.settle(child, q, q)
        gather.settle(1 - child, q, per + q, True)

    @pl.when(is_mid)
    def _():
        for q in range(per):
            cross(q).wait_send()
            onward(q).wait_send()
        for p in range(pieces):
            for i in range(1, 3):
                line(i, p).wait_send()

    @pl.when(is_end)
    def _():
        for p in range(pieces):
            line(0, p).wait_send()


def root_part(place_idx, update, given, root_upper, cid):
    depth, width = root_upper.shape
    per = update.shape[0] // BLK
    pieces = width // PIECE
    loads = depth // CHUNK
    vmem = pl.BlockSpec(memory_space=pltpu.VMEM)
    dma = pltpu.SemaphoreType.DMA
    low = jnp.bfloat16
    return pl.pallas_call(
        root_kernel,
        out_shape=jax.ShapeDtypeStruct((loads, CHUNK, BLK), low),
        in_specs=[
            pl.BlockSpec(memory_space=pltpu.SMEM), vmem, vmem, pl.BlockSpec(memory_space=pl.ANY),
        ],
        out_specs=vmem,
        scratch_shapes=[
            pltpu.VMEM((depth, width), low),
            pltpu.VMEM((per, BLK, BLK), low),
            pltpu.VMEM((2, 8 * per, BLK, BLK), low),
            pltpu.VMEM((BLK, depth), low),
            pltpu.VMEM((pieces, PIECE, BLK), low),
            pltpu.VMEM((pieces, PIECE, BLK), low),
            pltpu.VMEM((pieces, PIECE, BLK), low),
            pltpu.VMEM((pieces, PIECE, BLK), low),
            pltpu.VMEM((pieces, PIECE, BLK), low),
            pltpu.VMEM((pieces, PIECE, BLK), low),
            pltpu.VMEM((loads, CHUNK, BLK), jnp.float32),
        ]
        + plane_scratch(loads, False)
        + [
            dma((2, per)), dma((3, per)), dma((8, 2 * per)), dma((8, 2 * per)),
            dma((2, 3, pieces)), dma((loads,)),
        ],
        compiler_params=pltpu.CompilerParams(
            collective_id=cid, has_side_effects=True, vmem_limit_bytes=VMEM
        ),
    )(place_idx, update.reshape(per, BLK, BLK), given, root_upper)


def up_kernel(
    pick_ref, rows_ref, low_ref, coupling_ref, inverse_ref, both_ref,
    c_ref, a_ref, picked_ref, foreign_ref, home_ref, chain_ref, p_ref, acc_ref, part_ref, pair_ref,
    o_ref, w_ref, r_ref, send, recv, pick_sem, final_sem, c_sem, a_sem,
):
    me = lax.axis_index("col")
    place = lax.axis_index("row")
    child = place >> 1
    is_mid = ((place + 1) >> 1) == 1
    is_end = ((place + 1) >> 1) != 1
    per = picked_ref.shape[1]
    chunks = low_ref.shape[0]
    finals = part_ref.shape[0]
    size = part_ref.shape[1]

    whole = pltpu.make_async_copy(coupling_ref, c_ref, c_sem)
    whole.start()

    def load(j):
        rows = pl.ds(pl.multiple_of(j * CHUNK, CHUNK), CHUNK)
        return pltpu.make_async_copy(inverse_ref.at[rows], a_ref.at[j], a_sem.at[j])

    for j in range(chunks):
        load(j).start()
    enter(
        [{"col": me ^ (1 << b)} for b in range(3)] + [{"row": place ^ 1}, {"row": place ^ 3}]
    )

    def pick(q, k):
        i = pick_ref[k * per + q]
        block = rows_ref[jnp.maximum(i, 0)].astype(jnp.float32)
        picked_ref[k, q] = jnp.where(i >= 0, block, 0.0).astype(jnp.bfloat16)

    def hop(i, q):
        src, dst, flip = (
            (picked_ref.at[1 - child, q], foreign_ref.at[q], 1),
            (picked_ref.at[child, q], home_ref.at[q], 1),
            (picked_ref.at[1 - child, q], chain_ref.at[q], 3),
            (picked_ref.at[child, q], home_ref.at[q], 1),
        )[i]
        return row_copy(place, flip, src, dst, pick_sem.at[0, i, q], pick_sem.at[1, i if i < 3 else 1, q])

    for q in range(per):
        pick(q, 1 - child)
        pl.when(is_end)(lambda: hop(0, q).start())
    for q in range(per):
        pick(q, child)
        pl.when(is_end)(lambda: hop(1, q).start())

    @pl.when(is_mid)
    def _():
        for q in range(per):
            hop(0, q).wait_recv()
            picked_ref[1 - child, q] = f32_sum(picked_ref[1 - child, q], foreign_ref[q]).astype(
                jnp.bfloat16
            )
            hop(2, q).start()
        for q in range(per):
            hop(2, q).wait_recv()
            picked_ref[child, q] = f32_sum(picked_ref[child, q], chain_ref[q]).astype(jnp.bfloat16)
            hop(3, q).start()

    for q in range(per):
        hop(1, q).wait_recv()
        p_ref[:, q * BLK : (q + 1) * BLK] = f32_sum(picked_ref[child, q], home_ref[q]).T.astype(
            jnp.bfloat16
        )
    whole.wait()

    def produce(j):
        columns = pl.ds(pl.multiple_of(j * CHUNK, CHUNK), CHUNK)
        out = jnp.dot(p_ref[...], c_ref[:, columns], preferred_element_type=jnp.float32)
        return out.T.astype(jnp.bfloat16)

    def own(j, at, value):
        return low_ref[j, at].astype(jnp.float32) - value

    def consume(j):
        load(j).wait()
        value = jnp.dot(o_ref[j].T, a_ref[j], preferred_element_type=jnp.float32)

        @pl.when(j == 0)
        def _():
            acc_ref[...] = value

        @pl.when(j > 0)
        def _():
            acc_ref[...] += value

    PlaneSum(me, chunks, w_ref, r_ref, o_ref, send, recv).run(produce, own, consume, UP_LAGS)

    def final(i, p):
        if i == 0:
            return row_copy(
                place, 1, part_ref.at[p], pair_ref.at[p], final_sem.at[0, p], final_sem.at[1, p]
            )
        at = both_ref.at[child if i == 1 else 1 - child, p]
        return row_copy(
            place, 3 if i == 1 else 1, at, at, final_sem.at[1 + i, p], final_sem.at[4, p]
        )

    for p in range(finals):
        part_ref[p] = acc_ref[:, p * size : (p + 1) * size].T.astype(jnp.bfloat16)
        final(0, p).start()

    def relay(p):
        final(1, p).wait_recv()
        pl.when(is_mid)(lambda: final(2, p).start())

    for p in range(finals):
        final(0, p).wait_recv()
        both_ref[child, p] = f32_sum(part_ref[p], pair_ref[p]).astype(jnp.bfloat16)
        pl.when(is_mid)(lambda: final(1, p).start())
        if p >= 2:
            pl.when(is_mid)(functools.partial(relay, p - 2))
    for p in range(finals):
        if p < finals - 2:
            pl.when(is_end)(functools.partial(relay, p))
        else:
            relay(p)
    for p in range(finals):
        final(0, p).wait_send()

    @pl.when(is_mid)
    def _():
        for p in range(finals):
            final(1, p).wait_send()
            final(2, p).wait_send()
        for q in range(per):
            hop(2, q).wait_send()
            hop(3, q).wait_send()

    @pl.when(is_end)
    def _():
        for q in range(per):
            hop(0, q).wait_send()
            hop(1, q).wait_send()


UP_LAGS = (0, 3, 9, 14, 18, 22, 25)


def up_part(pick_idx, rows_low, child_low, coupling, child_inverse, cid):
    rows, width = child_inverse.shape
    coupled = coupling.shape[0]
    per = coupled // BLK
    chunks = rows // CHUNK
    finals = width // 256
    vmem = pl.BlockSpec(memory_space=pltpu.VMEM)
    anywhere = pl.BlockSpec(memory_space=pl.ANY)
    dma = pltpu.SemaphoreType.DMA
    low = jnp.bfloat16
    return pl.pallas_call(
        up_kernel,
        out_shape=jax.ShapeDtypeStruct((2, finals, width // finals, BLK), low),
        in_specs=[pl.BlockSpec(memory_space=pltpu.SMEM), vmem, vmem, anywhere, anywhere],
        out_specs=vmem,
        scratch_shapes=[
            pltpu.VMEM((coupled, rows), low),
            pltpu.VMEM((chunks, CHUNK, width), low),
            pltpu.VMEM((2, per, BLK, BLK), low),
            pltpu.VMEM((per, BLK, BLK), low),
            pltpu.VMEM((per, BLK, BLK), low),
            pltpu.VMEM((per, BLK, BLK), low),
            pltpu.VMEM((BLK, coupled), low),
            pltpu.VMEM((BLK, width), jnp.float32),
            pltpu.VMEM((finals, width // finals, BLK), low),
            pltpu.VMEM((finals, width // finals, BLK), low),
            pltpu.VMEM((chunks, CHUNK, BLK), low),
        ]
        + plane_scratch(chunks, False)
        + [dma((2, 4, per)), dma((5, finals)), dma, dma((chunks,))],
        compiler_params=pltpu.CompilerParams(
            collective_id=cid, has_side_effects=True, vmem_limit_bytes=VMEM
        ),
    )(pick_idx, rows_low, child_low, coupling, child_inverse)


def finish_kernel(x_ref, rows_ref, o_ref, root_ref, own_ref, sem):
    own = own_ref.shape[0]
    copy = pltpu.make_async_copy(
        rows_ref.at[pl.ds(pl.multiple_of(lax.axis_index("col") * own, own), own)], own_ref, sem
    )
    copy.start()
    step = 64

    def body(i, _):
        rows = pl.ds(pl.multiple_of(i * step, step), step)
        for k in range(2):
            o_ref[rows, k, :] = x_ref[k, rows, :].astype(jnp.float32)
        return 0

    lax.fori_loop(0, o_ref.shape[0] // step, body, 0, unroll=4)
    copy.wait()
    root_ref[...] = own_ref[...].astype(jnp.float32)


def local(row_devices, col_devices, child_inverse, root_upper, coupling, child_rhs, root_rhs, child_map):
    row_place = lax.axis_index("row")
    col_place = lax.axis_index("col")
    child_slot = row_place // (row_devices // 2)
    root_rows = root_upper.shape[0]
    coupled = coupling.shape[0]
    rhs_width = child_rhs.shape[2]
    vmem = pl.BlockSpec(memory_space=pltpu.VMEM)
    smem = pl.BlockSpec(memory_space=pltpu.SMEM)
    row_bits = list(range(bits_of(row_devices)))
    col_bits = list(range(bits_of(col_devices)))
    col_orders = [col_bits, col_bits[:1] + col_bits[:0:-1]] * 2
    row_orders = [row_bits, row_bits[::-1]] * 2
    pick_order = [row_bits[-1:] + row_bits[:-1]]
    contract_first = (((0,), (0,)), ((), ()))

    per_col = coupled // BLK
    root_blocks = root_rows // BLK
    local_map = lax.dynamic_slice_in_dim(child_map, col_place * per_col, per_col, 1)
    target = local_map - row_place * root_blocks
    block_hits = target[:, :, None] == jnp.arange(root_blocks, dtype=jnp.int32)[None, None, :]
    slots = jnp.arange(2 * per_col, dtype=jnp.int32).reshape(2, per_col, 1)
    place_idx = jnp.max(jnp.where(block_hits, slots, -1), axis=1)
    pick_idx = jnp.where((target >= 0) & (target < root_blocks), target, -1).reshape(-1)
    rhs_rows = root_rhs.shape[0]
    given_rows = lax.dynamic_update_slice(
        jnp.zeros((root_rows, rhs_width), jnp.float32),
        root_rhs,
        (col_place * rhs_rows, jnp.int32(0)),
    )

    own_rhs = lax.dynamic_index_in_dim(child_rhs, child_slot, 1, keepdims=False).astype(
        jnp.bfloat16
    )
    child_low = all_sum(
        jnp.dot(child_inverse, own_rhs, preferred_element_type=jnp.float32).astype(jnp.bfloat16),
        "col", col_devices, col_orders, 0,
    )
    update = jnp.dot(coupling, child_low, preferred_element_type=jnp.float32)
    update_both = both_sum(update.astype(jnp.bfloat16), "row", row_devices, 2, 1)
    root_term = pl.pallas_call(
        place_kernel,
        out_shape=jax.ShapeDtypeStruct((root_blocks, BLK, rhs_width), jnp.bfloat16),
        in_specs=[smem, vmem, vmem],
        out_specs=vmem,
    )(
        place_idx,
        update_both.reshape(2 * per_col, BLK, rhs_width),
        given_rows.reshape(root_blocks, BLK, rhs_width),
    )
    root_low = all_sum(
        root_term.reshape(root_rows, rhs_width), "col", col_devices, col_orders, 2
    )
    solved_low = all_sum(
        lax.dot_general(
            root_upper, root_low, contract_first, preferred_element_type=jnp.float32
        ).astype(jnp.bfloat16),
        "row", row_devices, row_orders, 3,
    )
    rows_low = all_sum(
        jnp.dot(root_upper, solved_low, preferred_element_type=jnp.float32).astype(jnp.bfloat16),
        "col", col_devices, col_orders, 4,
    )
    root_solution = lax.dynamic_slice_in_dim(rows_low, col_place * rhs_rows, rhs_rows, 0).astype(
        jnp.float32
    )
    picked = pl.pallas_call(
        pick_kernel,
        out_shape=jax.ShapeDtypeStruct((2 * per_col, BLK, rhs_width), jnp.bfloat16),
        in_specs=[smem, vmem],
        out_specs=vmem,
    )(pick_idx, rows_low.reshape(root_blocks, BLK, rhs_width))
    picked_half = all_sum(
        picked.reshape(2 * coupled, rhs_width), "row", row_devices, pick_order, 5,
        gathers=len(row_bits) - 1,
    )
    own_pick = lax.dynamic_slice_in_dim(picked_half, child_slot * coupled, coupled, 0)
    back_term = all_sum(
        lax.dot_general(
            coupling, own_pick, contract_first, preferred_element_type=jnp.float32
        ).astype(jnp.bfloat16),
        "col", col_devices, col_orders, 6,
    )
    adjusted = (child_low.astype(jnp.float32) - back_term.astype(jnp.float32)).astype(
        jnp.bfloat16
    )
    final_rows = lax.dot_general(
        child_inverse, adjusted, contract_first, preferred_element_type=jnp.float32
    )
    final_both = both_sum(final_rows.astype(jnp.bfloat16), "row", row_devices, 4, 7)
    child_solution = pl.pallas_call(
        weave_kernel,
        out_shape=jax.ShapeDtypeStruct(child_rhs.shape, jnp.float32),
        in_specs=[vmem],
        out_specs=vmem,
    )(final_both)
    return (root_solution, child_solution)


def near(row_devices, col_devices, child_inverse, root_upper, coupling, child_rhs, root_rhs, child_map):
    row_place = lax.axis_index("row")
    col_place = lax.axis_index("col")
    child_slot = row_place // (row_devices // 2)
    root_rows = root_upper.shape[0]
    coupled = coupling.shape[0]
    rhs_width = child_rhs.shape[2]
    vmem = pl.BlockSpec(memory_space=pltpu.VMEM)

    per_col = coupled // BLK
    root_blocks = root_rows // BLK
    local_map = lax.dynamic_slice_in_dim(child_map, col_place * per_col, per_col, 1)
    target = local_map - row_place * root_blocks
    block_hits = (child_map - row_place * root_blocks)[:, :, None] == jnp.arange(root_blocks, dtype=jnp.int32)[None, None, :]
    slots = jnp.arange(child_map.shape[1], dtype=jnp.int32).reshape(1, -1, 1)
    place_idx = jnp.max(jnp.where(block_hits, slots, -1), axis=1)
    pick_idx = jnp.where((target >= 0) & (target < root_blocks), target, -1).reshape(-1)

    own_rhs = lax.dynamic_index_in_dim(child_rhs, child_slot, 1, keepdims=False).astype(
        jnp.bfloat16
    )
    child_low, update, given = down(child_inverse, coupling, own_rhs, root_rhs, 0)
    rows_low = root_part(place_idx, update, given, root_upper, 1)
    both = up_part(
        pick_idx, rows_low.reshape(root_blocks, BLK, rhs_width), child_low, coupling,
        child_inverse, 2,
    )
    anywhere = pl.BlockSpec(memory_space=pl.ANY)
    child_solution, root_solution = pl.pallas_call(
        finish_kernel,
        out_shape=(
            jax.ShapeDtypeStruct(child_rhs.shape, jnp.float32),
            jax.ShapeDtypeStruct(root_rhs.shape, jnp.float32),
        ),
        in_specs=[vmem, anywhere],
        out_specs=(vmem, vmem),
        scratch_shapes=[
            pltpu.VMEM(root_rhs.shape, jnp.bfloat16), pltpu.SemaphoreType.DMA,
        ],
    )(both.reshape(2, -1, rhs_width), rows_low.reshape(-1, rhs_width))
    return (root_solution, child_solution)


def solution(mesh):
    body = near if (mesh.shape["row"], mesh.shape["col"]) == (4, 8) else local
    return jax.shard_map(
        functools.partial(body, mesh.shape["row"], mesh.shape["col"]),
        mesh=mesh,
        in_specs=(
            P("row", "col"),
            P("row", "col"),
            P("col", "row"),
            P("col", None, None),
            P(("row", "col"), None),
            P(),
        ),
        out_specs=(P(("row", "col"), None), P("col", None, None)),
        check_vma=False,
    )
```

```python
import functools

import jax
import jax.numpy as jnp
from jax import lax
from jax.experimental import pallas as pl
from jax.experimental.pallas import tpu as pltpu
from jax.sharding import PartitionSpec as P

BLK = 128
MESH = pl.DeviceIdType.MESH
VMEM = 58 * 2**20


def bits_of(n):
    m = n.bit_length() - 1
    assert 1 << m == n
    return m


def greet(axis, me, bits):
    barrier = pltpu.get_barrier_semaphore()
    for b in bits:
        pl.semaphore_signal(
            barrier, inc=1, device_id={axis: me ^ (1 << b)}, device_id_type=MESH
        )
    pl.semaphore_wait(barrier, len(bits))


def remote(axis, me, bit, src, dst, send, recv):
    copy = pltpu.make_async_remote_copy(
        src_ref=src,
        dst_ref=dst,
        send_sem=send,
        recv_sem=recv,
        device_id={axis: me ^ (1 << bit)},
        device_id_type=MESH,
    )
    copy.start()
    return copy


def run_streams(streams, steps, begin, finish):
    copies = [[begin(s, 0)] for s in range(streams)]
    for t in range(steps):
        for s in range(streams):
            copies[s][t].wait_recv()
            finish(s, t)
            if t + 1 < steps:
                copies[s].append(begin(s, t + 1))
    for own in copies:
        for copy in own:
            copy.wait_send()


def spans(me, order, n):
    low = jnp.int32(0)
    size = n
    offset = 0
    out = []
    for b in order:
        half = size // 2
        mine = (me >> b) & 1
        keep, away = low + mine * half, low + (1 - mine) * half
        out.append((keep, away, half, offset))
        low, size, offset = keep, half, offset + half
    return out


def add_landed(s, span, src, r_ref, put):
    keep, _, half, offset = span

    def add(i, _):
        total = src[s, keep + i].astype(jnp.float32) + r_ref[s, offset + i].astype(jnp.float32)
        put(keep + i, total.astype(jnp.bfloat16))
        return 0

    lax.fori_loop(0, half, add, 0)


def all_sum_kernel(axis, n, orders, gathers, x_ref, o_ref, w_ref, r_ref, send, recv):
    me = lax.axis_index(axis)
    steps = len(orders[0])
    plans = [spans(me, order, n) for order in orders]
    greet(axis, me, list(range(steps)))

    def begin(s, t):
        if t < steps:
            _, away, half, offset = plans[s][t]
            src = (x_ref if t == 0 else w_ref).at[s, pl.ds(away, half)]
            dst = r_ref.at[s, pl.ds(offset, half)]
            bit = orders[s][t]
        else:
            back = 2 * steps - 1 - t
            src = dst = o_ref.at[s, pl.ds(plans[s][back][0], plans[s][back][2])]
            bit = orders[s][back]
        return remote(axis, me, bit, src, dst, send.at[s, t], recv.at[s, t])

    def finish(s, t):
        if t < steps:

            def put(place, value):
                if t == steps - 1:
                    o_ref[s, place] = value
                else:
                    w_ref[s, place] = value

            add_landed(s, plans[s][t], x_ref if t == 0 else w_ref, r_ref, put)

    run_streams(len(orders), steps + gathers, begin, finish)


def all_sum(x, axis, n, orders, cid, gathers=None):
    rows, width = x.shape
    m = bits_of(n)
    gathers = m if gathers is None else gathers
    streams = len(orders)
    shape = (streams, n, rows // (streams * n), width)
    out = pl.pallas_call(
        functools.partial(all_sum_kernel, axis, n, orders, gathers),
        out_shape=jax.ShapeDtypeStruct(shape, jnp.bfloat16),
        in_specs=[pl.BlockSpec(memory_space=pltpu.VMEM)],
        out_specs=pl.BlockSpec(memory_space=pltpu.VMEM),
        scratch_shapes=[
            pltpu.VMEM(shape, jnp.bfloat16),
            pltpu.VMEM(shape, jnp.bfloat16),
            pltpu.SemaphoreType.DMA((streams, 2 * m)),
            pltpu.SemaphoreType.DMA((streams, 2 * m)),
        ],
        compiler_params=pltpu.CompilerParams(collective_id=cid, has_side_effects=True),
    )(x.reshape(shape))
    return out.reshape(rows, width)


def both_sum_kernel(axis, n, streams, x_ref, o_ref, w_ref, r_ref, send, recv):
    me = lax.axis_index(axis)
    m = bits_of(n)
    slot = me >> (m - 1)
    plan = spans(me, list(range(m - 1)), n // 2)
    greet(axis, me, list(range(m)))

    def begin(s, t):
        if t < m - 1:
            _, away, half, offset = plan[t]
            src = (x_ref if t == 0 else w_ref).at[s, pl.ds(away, half)]
            dst = r_ref.at[s, pl.ds(offset, half)]
            bit = t
        elif t == m - 1:
            src = dst = o_ref.at[slot, s, pl.ds(plan[-1][0], 1)]
            bit = m - 1
        else:
            bit = 2 * (m - 1) - t
            src = dst = o_ref.at[:, s, pl.ds(plan[bit][0], plan[bit][2])]
        return remote(axis, me, bit, src, dst, send.at[s, t], recv.at[s, t])

    def finish(s, t):
        if t < m - 1:

            def put(place, value):
                if t == m - 2:
                    o_ref[slot, s, place] = value
                else:
                    w_ref[s, place] = value

            add_landed(s, plan[t], x_ref if t == 0 else w_ref, r_ref, put)

    run_streams(streams, 2 * m - 1, begin, finish)


def both_sum(x, axis, n, streams, cid):
    rows, width = x.shape
    m = bits_of(n)
    half = n // 2
    shape = (streams, half, rows // (streams * half), width)
    out = pl.pallas_call(
        functools.partial(both_sum_kernel, axis, n, streams),
        out_shape=jax.ShapeDtypeStruct((2,) + shape, jnp.bfloat16),
        in_specs=[pl.BlockSpec(memory_space=pltpu.VMEM)],
        out_specs=pl.BlockSpec(memory_space=pltpu.VMEM),
        scratch_shapes=[
            pltpu.VMEM(shape, jnp.bfloat16),
            pltpu.VMEM(shape, jnp.bfloat16),
            pltpu.SemaphoreType.DMA((streams, 2 * m)),
            pltpu.SemaphoreType.DMA((streams, 2 * m)),
        ],
        compiler_params=pltpu.CompilerParams(collective_id=cid, has_side_effects=True),
    )(x.reshape(shape))
    return out.reshape(2, rows, width)


def place_kernel(idx_ref, update_ref, given_ref, o_ref):
    def body(j, _):
        value = given_ref[j]
        for k in range(2):
            i = idx_ref[k, j]
            block = update_ref[jnp.maximum(i, 0)].astype(jnp.float32)
            value = value - jnp.where(i >= 0, block, 0.0)
        o_ref[j] = value.astype(jnp.bfloat16)
        return 0

    lax.fori_loop(0, o_ref.shape[0], body, 0)


def pick_kernel(idx_ref, rows_ref, o_ref):
    def body(j, _):
        i = idx_ref[j]
        block = rows_ref[jnp.maximum(i, 0)].astype(jnp.float32)
        o_ref[j] = jnp.where(i >= 0, block, 0.0).astype(jnp.bfloat16)
        return 0

    lax.fori_loop(0, o_ref.shape[0], body, 0)


def weave_kernel(x_ref, o_ref):
    step = 64

    def body(i, _):
        rows = pl.ds(pl.multiple_of(i * step, step), step)
        for k in range(2):
            o_ref[rows, k, :] = x_ref[k, rows, :].astype(jnp.float32)
        return 0

    lax.fori_loop(0, o_ref.shape[0] // step, body, 0)


CHUNK = 512
FAR = (0, 2, 6, 10, 14, 18, 20)


class PlaneSum:
    def __init__(self, me, chunks, w_ref, r_ref, o_ref, send, recv):
        self.me, self.chunks = me, chunks
        self.w, self.r, self.o = w_ref, r_ref, o_ref
        self.send, self.recv = send, recv

    def bits(self, j):
        first = 1 + j % 2
        return 0, first, 3 - first

    def keeps(self, j):
        low, size, out = 0, CHUNK, []
        for b in self.bits(j):
            size = size // 2
            mine = (self.me >> b) & 1
            out.append((low + mine * size, low + (1 - mine) * size, size))
            low = low + mine * size
        return out

    def copy(self, s, j):
        bits, keeps = self.bits(j), self.keeps(j)
        if s < 3:
            _, away, size = keeps[s]
            src = self.w.at[j, pl.ds(pl.multiple_of(away, size), size)]
            dst = self.r.at[j, pl.ds(CHUNK - 2 * size, size)]
            bit = bits[s]
        else:
            keep, _, size = keeps[5 - s]
            src = dst = self.o.at[j, pl.ds(pl.multiple_of(keep, size), size)]
            bit = bits[5 - s]
        return pltpu.make_async_remote_copy(
            src_ref=src,
            dst_ref=dst,
            send_sem=self.send.at[s, j],
            recv_sem=self.recv.at[s, j],
            device_id={"col": self.me ^ (1 << bit)},
            device_id_type=MESH,
        )

    def total(self, s, j, low, size):
        keep, _, half = self.keeps(j)[s]
        mine = self.w[j, pl.ds(pl.multiple_of(keep + low, size), size)].astype(jnp.float32)
        landed = self.r[j, pl.ds(pl.multiple_of(CHUNK - 2 * half + low, size), size)]
        return mine + landed.astype(jnp.float32)

    def fold(self, s, j):
        self.copy(s, j).wait_recv()
        keep, _, half = self.keeps(j)[s]
        size = half // 2
        stay = ((self.me >> self.bits(j)[s + 1]) & 1) * size
        for low, last in ((size - stay, False), (stay, True)):
            self.w[j, pl.ds(pl.multiple_of(keep + low, size), size)] = self.total(
                s, j, low, size
            ).astype(jnp.bfloat16)
            if not last:
                self.copy(s + 1, j).start()

    def run(self, produce, own, consume, lags=FAR, beside=()):
        def stage(k, j):
            if k == 0:
                self.w[j] = produce(j)
                self.copy(0, j).start()
            elif k < 3:
                self.fold(k - 1, j)
            elif k == 3:
                self.copy(2, j).wait_recv()
                keep, _, size = self.keeps(j)[2]
                place = pl.ds(pl.multiple_of(keep, size), size)
                self.o[j, place] = own(j, place, self.total(2, j, 0, size)).astype(jnp.bfloat16)
                self.copy(3, j).start()
            else:
                self.copy(k - 1, j).wait_recv()
                if k < 6:
                    self.copy(k, j).start()
                else:
                    consume(j)

        def tick(t, _):
            for k in reversed(range(7)):
                j = t - lags[k]
                pl.when((j >= 0) & (j < self.chunks))(functools.partial(stage, k, j))
            for at, act in beside:
                pl.when(t == at)(act)
            return 0

        lax.fori_loop(0, self.chunks + lags[-1], tick, 0)

        def settle(j, _):
            for s in range(6):
                self.copy(s, j).wait_send()
            return 0

        lax.fori_loop(0, self.chunks, settle, 0)


def plane_scratch(chunks, with_out):
    out = [
        pltpu.VMEM((chunks, CHUNK, BLK), jnp.bfloat16),
        pltpu.VMEM((chunks, CHUNK, BLK), jnp.bfloat16),
    ]
    if with_out:
        out.append(pltpu.VMEM((chunks, CHUNK, BLK), jnp.bfloat16))
    return out + [pltpu.SemaphoreType.DMA((6, chunks)), pltpu.SemaphoreType.DMA((6, chunks))]


def enter(partners):
    barrier = pltpu.get_barrier_semaphore()
    for partner in partners:
        pl.semaphore_signal(barrier, inc=1, device_id=partner, device_id_type=MESH)
    pl.semaphore_wait(barrier, len(partners))


class PlaneGather:
    def __init__(self, me, ref, count, send, recv):
        self.me, self.ref, self.count, self.send, self.recv = me, ref, count, send, recv

    def copy(self, i, k, q, slot, direct=False):
        far = ((0, 2), (0, 4), (2, 4), (4, 2), (0, 1), (2, 1), (4, 1), (6, 1))[i]
        low, size = ((i - 2) * (BLK // 2), BLK // 2) if i in (2, 3) else (0, BLK)
        if direct and i == 2:
            far, size = (0, 6), BLK
        part = self.ref.at[k, self.count * (self.me ^ far[0]) + q, pl.ds(low, size)]
        return pltpu.make_async_remote_copy(
            src_ref=part,
            dst_ref=part,
            send_sem=self.send.at[i, slot],
            recv_sem=self.recv.at[i, slot],
            device_id={"col": self.me ^ far[1]},
            device_id_type=MESH,
        )

    def begin(self, k, q, slot, direct=False):
        for i in (0, 1, 2, 4) if direct else (0, 1, 4):
            self.copy(i, k, q, slot, direct).start()

    def relay(self, k, q, slot, direct=False):
        for i in (0, 1):
            self.copy(i, k, q, slot).wait_recv()
            if not direct:
                self.copy(i + 2, k, q, slot).start()
            self.copy(i + 5, k, q, slot).start()

    def across(self, k, q, slot, direct=False):
        self.copy(2, k, q, slot, direct).wait_recv()
        if not direct:
            self.copy(3, k, q, slot).wait_recv()
        self.copy(7, k, q, slot).start()

    def land(self, *at):
        for i in range(4, 8):
            self.copy(i, *at).wait_recv()

    def settle(self, k, q, slot, direct=False):
        for i in range(8):
            if not (direct and i == 3):
                self.copy(i, k, q, slot, direct).wait_send()


def row_copy(place, flip, src, dst, send, recv):
    return pltpu.make_async_remote_copy(
        src_ref=src,
        dst_ref=dst,
        send_sem=send,
        recv_sem=recv,
        device_id={"row": place ^ flip},
        device_id_type=MESH,
    )


def f32_sum(*terms):
    total = terms[0].astype(jnp.float32)
    for term in terms[1:]:
        total = total + term.astype(jnp.float32)
    return total


AHEAD = 3
RELAY, ACROSS = 4, 8


def down_kernel(
    chunks, inverse_ref, coupling_ref, rhs_ref, root_ref, low_ref, update_ref, given_ref,
    a_ref, c_ref, acc_ref, w_ref, r_ref, send, recv, a_sem, c_sem, given_send, given_recv,
    wide_ref, b_ref, rhs_sem,
):
    me = lax.axis_index("col")

    def load(j):
        return pltpu.make_async_copy(
            inverse_ref.at[pl.ds(pl.multiple_of(j * CHUNK, CHUNK), CHUNK)],
            a_ref.at[j],
            a_sem.at[j],
        )

    right = pltpu.make_async_copy(
        rhs_ref.at[:, lax.axis_index("row") >> 1], wide_ref, rhs_sem
    )
    right.start()
    for j in range(AHEAD):
        load(j).start()
    enter([{"col": me ^ (1 << b)} for b in range(3)])
    mine = root_ref.shape[0] // BLK
    given = PlaneGather(me, given_ref, mine, given_send, given_recv)
    for q in range(mine):
        given_ref[0, mine * me + q] = root_ref[pl.ds(q * BLK, BLK)].astype(jnp.bfloat16)
        given.begin(0, q, q)
    right.wait()
    b_ref[...] = wide_ref[...].astype(jnp.bfloat16)
    acc_ref[...] = jnp.zeros_like(acc_ref)
    whole = pltpu.make_async_copy(coupling_ref, c_ref, c_sem)

    def produce(j):
        load(j).wait()

        @pl.when(j + AHEAD < chunks)
        def _():
            load(j + AHEAD).start()

        @pl.when(j + AHEAD == chunks)
        def _():
            whole.start()

        return jnp.dot(a_ref[j], b_ref[...], preferred_element_type=jnp.float32).astype(
            jnp.bfloat16
        )

    def consume(j):
        @pl.when(j == 0)
        def _():
            whole.wait()

        columns = pl.ds(pl.multiple_of(j * CHUNK, CHUNK), CHUNK)
        acc_ref[...] += jnp.dot(
            c_ref[:, columns], low_ref[j], preferred_element_type=jnp.float32
        )

    def each(act):
        return lambda: [act(0, q, q) for q in range(mine)] and None

    PlaneSum(me, chunks, w_ref, r_ref, low_ref, send, recv).run(
        produce,
        lambda j, place, value: value,
        consume,
        beside=((RELAY, each(given.relay)), (ACROSS, each(given.across))),
    )
    each(given.land)()
    each(given.settle)()
    update_ref[...] = acc_ref[...].astype(jnp.bfloat16)


def down(child_inverse, coupling, child_rhs, root_rhs, cid):
    rows, depth = child_inverse.shape
    chunks = rows // CHUNK
    coupled = coupling.shape[0]
    vmem = pl.BlockSpec(memory_space=pltpu.VMEM)
    anywhere = pl.BlockSpec(memory_space=pl.ANY)
    mine = root_rhs.shape[0] // BLK
    return pl.pallas_call(
        functools.partial(down_kernel, chunks),
        out_shape=(
            jax.ShapeDtypeStruct((chunks, CHUNK, BLK), jnp.bfloat16),
            jax.ShapeDtypeStruct((coupled, BLK), jnp.bfloat16),
            jax.ShapeDtypeStruct((1, 8 * mine, BLK, BLK), jnp.bfloat16),
        ),
        in_specs=[anywhere, anywhere, anywhere, vmem],
        out_specs=(vmem, vmem, vmem),
        scratch_shapes=[
            pltpu.VMEM((chunks, CHUNK, depth), jnp.bfloat16),
            pltpu.VMEM((coupled, rows), jnp.bfloat16),
            pltpu.VMEM((coupled, BLK), jnp.float32),
        ]
        + plane_scratch(chunks, False)
        + [pltpu.SemaphoreType.DMA((chunks,)), pltpu.SemaphoreType.DMA]
        + [pltpu.SemaphoreType.DMA((8, mine))] * 2
        + [
            pltpu.VMEM((depth, BLK), jnp.float32),
            pltpu.VMEM((depth, BLK), jnp.bfloat16),
            pltpu.SemaphoreType.DMA,
        ],
        compiler_params=pltpu.CompilerParams(
            collective_id=cid, has_side_effects=True, vmem_limit_bytes=VMEM
        ),
    )(child_inverse, coupling, child_rhs, root_rhs)


PIECE = 256
LINE_LAGS = (0, 2, 4)
ROOT_LAGS = (0, 4, 11, 17, 23, 29, 33)


def root_kernel(
    map_ref, update_ref, given_ref, upper_ref, rows_ref,
    u_ref, pair_ref, up_ref, x_ref, y_ref, outer_ref, mid_ref, inward_ref, outward_ref, fin_ref,
    acc_ref,
    w_ref, r_ref, send, recv,
    pair_sem, cross_sem, up_send, up_recv, line_sem, u_sem,
):
    me = lax.axis_index("col")
    place = lax.axis_index("row")
    child = place >> 1
    is_mid = ((place + 1) >> 1) == 1
    is_end = ((place + 1) >> 1) != 1
    blocks = given_ref.shape[1]
    per = update_ref.shape[0]
    depth, width = upper_ref.shape
    loads = depth // CHUNK

    def load(i):
        rows = pl.ds(i * CHUNK, CHUNK)
        return pltpu.make_async_copy(upper_ref.at[rows], u_ref.at[rows], u_sem.at[i])

    for i in range(loads):
        load(i).start()
    enter(
        [{"col": me ^ b} for b in (1, 2, 4, 6)] + [{"row": place ^ 1}, {"row": place ^ 3}]
    )

    def pair(q):
        return row_copy(
            place, 1, update_ref.at[q], pair_ref.at[q], pair_sem.at[0, q], pair_sem.at[1, q]
        )

    def cross(q):
        part = up_ref.at[child, per * me + q]
        return row_copy(place, 3, part, part, cross_sem.at[0, q], cross_sem.at[1, q])

    def onward(q):
        part = up_ref.at[1 - child, per * me + q]
        return row_copy(place, 1, part, part, cross_sem.at[2, q], cross_sem.at[1, q])

    for q in range(per):
        pair(q).start()
    gather = PlaneGather(me, up_ref, per, up_send, up_recv)
    for q in range(per):
        pair(q).wait_recv()
        up_ref[child, per * me + q] = f32_sum(update_ref[q], pair_ref[q]).astype(jnp.bfloat16)
        pl.when(is_mid)(lambda: cross(q).start())
        gather.begin(child, q, q)
    for q in range(per):
        cross(q).wait_recv()
        pl.when(is_mid)(lambda: onward(q).start())
        gather.begin(1 - child, q, per + q, True)
        gather.relay(child, q, q)
    for q in range(per):
        gather.across(child, q, q)
    for q in range(per):
        gather.relay(1 - child, q, per + q, True)
        gather.across(1 - child, q, per + q, True)
    for q in range(per):
        gather.land(child, q, q)
        gather.land(1 - child, q, per + q)

    def put(j, _):
        value = given_ref[0, j].astype(jnp.float32)
        for k in range(2):
            i = map_ref[k, j]
            block = up_ref[k, jnp.maximum(i, 0)].astype(jnp.float32)
            value = value - jnp.where(i >= 0, block, 0.0)
        x_ref[:, pl.ds(pl.multiple_of(j * BLK, BLK), BLK)] = value.T.astype(jnp.bfloat16)
        return 0

    lax.fori_loop(0, blocks, put, 0, unroll=4)

    pieces = width // PIECE

    def line(i, p):
        src, dst, flip = (
            (y_ref.at[p], outer_ref.at[p], 1),
            (inward_ref.at[p], mid_ref.at[p], 3),
            (outward_ref.at[p], outer_ref.at[p], 1),
        )[i]
        return row_copy(place, flip, src, dst, line_sem.at[0, i, p], line_sem.at[1, i % 2, p])

    for i in range(loads):
        load(i).wait()
    def tile(t):
        columns = pl.ds(pl.multiple_of(t * CHUNK, CHUNK), CHUNK)
        out = jnp.dot(x_ref[...], u_ref[:, columns], preferred_element_type=jnp.float32)
        out = out.T.astype(jnp.bfloat16)
        for i in range(CHUNK // PIECE):
            y_ref[t * (CHUNK // PIECE) + i] = out[i * PIECE : (i + 1) * PIECE]

            @pl.when(is_end)
            def _():
                line(0, t * (CHUNK // PIECE) + i).start()

    def line_stage(s, p):
        if s == 0:

            @pl.when(is_mid)
            def _():
                line(0, p).wait_recv()
                inward_ref[p] = f32_sum(y_ref[p], outer_ref[p]).astype(jnp.bfloat16)
                line(1, p).start()

        elif s == 1:

            @pl.when(is_mid)
            def _():
                line(1, p).wait_recv()
                both = f32_sum(y_ref[p], mid_ref[p])
                outward_ref[p] = both.astype(jnp.bfloat16)
                line(2, p).start()
                fin_ref[p] = (both + outer_ref[p].astype(jnp.float32)).astype(jnp.bfloat16)

        else:

            @pl.when(is_end)
            def _():
                line(2, p).wait_recv()
                fin_ref[p] = f32_sum(y_ref[p], outer_ref[p]).astype(jnp.bfloat16)

    group = CHUNK // PIECE
    groups = width // CHUNK

    def product(j, g):
        rows = pl.ds(pl.multiple_of(j * CHUNK, CHUNK), CHUNK)
        columns = pl.ds(g * CHUNK, CHUNK)
        part = fin_ref[pl.ds(g * group, group)].reshape(CHUNK, BLK)
        return jnp.dot(u_ref[rows, columns], part, preferred_element_type=jnp.float32)

    def add_group(g):
        def body(j, _):
            value = product(j, g)
            acc_ref[j] = value if g == 0 else acc_ref[j] + value
            return 0

        lax.fori_loop(0, loads, body, 0)

    for t in range(groups):
        tile(t)
    for t in range(pieces + LINE_LAGS[-1]):
        for s in range(3):
            if 0 <= t - LINE_LAGS[s] < pieces:
                line_stage(s, t - LINE_LAGS[s])
        done = t - LINE_LAGS[-1] + 1
        if done > 0 and done % group == 0 and done < pieces:
            add_group(done // group - 1)

    PlaneSum(me, loads, w_ref, r_ref, rows_ref, send, recv).run(
        lambda j: (acc_ref[j] + product(j, groups - 1)).astype(jnp.bfloat16),
        lambda j, at, value: value,
        lambda j: None,
        ROOT_LAGS,
    )

    for q in range(per):
        pair(q).wait_send()
        gather.settle(child, q, q)
        gather.settle(1 - child, q, per + q, True)

    @pl.when(is_mid)
    def _():
        for q in range(per):
            cross(q).wait_send()
            onward(q).wait_send()
        for p in range(pieces):
            for i in range(1, 3):
                line(i, p).wait_send()

    @pl.when(is_end)
    def _():
        for p in range(pieces):
            line(0, p).wait_send()


def root_part(place_idx, update, given, root_upper, cid):
    depth, width = root_upper.shape
    per = update.shape[0] // BLK
    pieces = width // PIECE
    loads = depth // CHUNK
    vmem = pl.BlockSpec(memory_space=pltpu.VMEM)
    dma = pltpu.SemaphoreType.DMA
    low = jnp.bfloat16
    return pl.pallas_call(
        root_kernel,
        out_shape=jax.ShapeDtypeStruct((loads, CHUNK, BLK), low),
        in_specs=[
            pl.BlockSpec(memory_space=pltpu.SMEM), vmem, vmem, pl.BlockSpec(memory_space=pl.ANY),
        ],
        out_specs=vmem,
        scratch_shapes=[
            pltpu.VMEM((depth, width), low),
            pltpu.VMEM((per, BLK, BLK), low),
            pltpu.VMEM((2, 8 * per, BLK, BLK), low),
            pltpu.VMEM((BLK, depth), low),
            pltpu.VMEM((pieces, PIECE, BLK), low),
            pltpu.VMEM((pieces, PIECE, BLK), low),
            pltpu.VMEM((pieces, PIECE, BLK), low),
            pltpu.VMEM((pieces, PIECE, BLK), low),
            pltpu.VMEM((pieces, PIECE, BLK), low),
            pltpu.VMEM((pieces, PIECE, BLK), low),
            pltpu.VMEM((loads, CHUNK, BLK), jnp.float32),
        ]
        + plane_scratch(loads, False)
        + [
            dma((2, per)), dma((3, per)), dma((8, 2 * per)), dma((8, 2 * per)),
            dma((2, 3, pieces)), dma((loads,)),
        ],
        compiler_params=pltpu.CompilerParams(
            collective_id=cid, has_side_effects=True, vmem_limit_bytes=VMEM
        ),
    )(place_idx, update.reshape(per, BLK, BLK), given, root_upper)


def up_kernel(
    pick_ref, rows_ref, low_ref, coupling_ref, inverse_ref, both_ref,
    c_ref, a_ref, picked_ref, foreign_ref, home_ref, chain_ref, p_ref, acc_ref, part_ref, pair_ref,
    o_ref, w_ref, r_ref, send, recv, pick_sem, final_sem, c_sem, a_sem,
):
    me = lax.axis_index("col")
    place = lax.axis_index("row")
    child = place >> 1
    is_mid = ((place + 1) >> 1) == 1
    is_end = ((place + 1) >> 1) != 1
    per = picked_ref.shape[1]
    chunks = low_ref.shape[0]
    finals = part_ref.shape[0]
    size = part_ref.shape[1]

    whole = pltpu.make_async_copy(coupling_ref, c_ref, c_sem)
    whole.start()

    def load(j):
        rows = pl.ds(pl.multiple_of(j * CHUNK, CHUNK), CHUNK)
        return pltpu.make_async_copy(inverse_ref.at[rows], a_ref.at[j], a_sem.at[j])

    for j in range(chunks):
        load(j).start()
    enter(
        [{"col": me ^ (1 << b)} for b in range(3)] + [{"row": place ^ 1}, {"row": place ^ 3}]
    )

    def pick(q, k):
        i = pick_ref[k * per + q]
        block = rows_ref[jnp.maximum(i, 0)].astype(jnp.float32)
        picked_ref[k, q] = jnp.where(i >= 0, block, 0.0).astype(jnp.bfloat16)

    def hop(i, q):
        src, dst, flip = (
            (picked_ref.at[1 - child, q], foreign_ref.at[q], 1),
            (picked_ref.at[child, q], home_ref.at[q], 1),
            (picked_ref.at[1 - child, q], chain_ref.at[q], 3),
            (picked_ref.at[child, q], home_ref.at[q], 1),
        )[i]
        return row_copy(place, flip, src, dst, pick_sem.at[0, i, q], pick_sem.at[1, i if i < 3 else 1, q])

    for q in range(per):
        pick(q, 1 - child)
        pl.when(is_end)(lambda: hop(0, q).start())
    for q in range(per):
        pick(q, child)
        pl.when(is_end)(lambda: hop(1, q).start())

    @pl.when(is_mid)
    def _():
        for q in range(per):
            hop(0, q).wait_recv()
            picked_ref[1 - child, q] = f32_sum(picked_ref[1 - child, q], foreign_ref[q]).astype(
                jnp.bfloat16
            )
            hop(2, q).start()
        for q in range(per):
            hop(2, q).wait_recv()
            picked_ref[child, q] = f32_sum(picked_ref[child, q], chain_ref[q]).astype(jnp.bfloat16)
            hop(3, q).start()

    for q in range(per):
        hop(1, q).wait_recv()
        p_ref[:, q * BLK : (q + 1) * BLK] = f32_sum(picked_ref[child, q], home_ref[q]).T.astype(
            jnp.bfloat16
        )
    whole.wait()

    def produce(j):
        columns = pl.ds(pl.multiple_of(j * CHUNK, CHUNK), CHUNK)
        out = jnp.dot(p_ref[...], c_ref[:, columns], preferred_element_type=jnp.float32)
        return out.T.astype(jnp.bfloat16)

    def own(j, at, value):
        return low_ref[j, at].astype(jnp.float32) - value

    def consume(j):
        load(j).wait()
        value = jnp.dot(o_ref[j].T, a_ref[j], preferred_element_type=jnp.float32)

        @pl.when(j == 0)
        def _():
            acc_ref[...] = value

        @pl.when(j > 0)
        def _():
            acc_ref[...] += value

    PlaneSum(me, chunks, w_ref, r_ref, o_ref, send, recv).run(produce, own, consume, UP_LAGS)

    def final(i, p):
        if i == 0:
            return row_copy(
                place, 1, part_ref.at[p], pair_ref.at[p], final_sem.at[0, p], final_sem.at[1, p]
            )
        at = both_ref.at[child if i == 1 else 1 - child, p]
        return row_copy(
            place, 3 if i == 1 else 1, at, at, final_sem.at[1 + i, p], final_sem.at[4, p]
        )

    for p in range(finals):
        part_ref[p] = acc_ref[:, p * size : (p + 1) * size].T.astype(jnp.bfloat16)
        final(0, p).start()

    def relay(p):
        final(1, p).wait_recv()
        pl.when(is_mid)(lambda: final(2, p).start())

    for p in range(finals):
        final(0, p).wait_recv()
        both_ref[child, p] = f32_sum(part_ref[p], pair_ref[p]).astype(jnp.bfloat16)
        pl.when(is_mid)(lambda: final(1, p).start())
        if p >= 2:
            pl.when(is_mid)(functools.partial(relay, p - 2))
    for p in range(finals):
        if p < finals - 2:
            pl.when(is_end)(functools.partial(relay, p))
        else:
            relay(p)
    for p in range(finals):
        final(0, p).wait_send()

    @pl.when(is_mid)
    def _():
        for p in range(finals):
            final(1, p).wait_send()
            final(2, p).wait_send()
        for q in range(per):
            hop(2, q).wait_send()
            hop(3, q).wait_send()

    @pl.when(is_end)
    def _():
        for q in range(per):
            hop(0, q).wait_send()
            hop(1, q).wait_send()


UP_LAGS = (0, 3, 9, 15, 21, 27, 31)


def up_part(pick_idx, rows_low, child_low, coupling, child_inverse, cid):
    rows, width = child_inverse.shape
    coupled = coupling.shape[0]
    per = coupled // BLK
    chunks = rows // CHUNK
    finals = width // 256
    vmem = pl.BlockSpec(memory_space=pltpu.VMEM)
    anywhere = pl.BlockSpec(memory_space=pl.ANY)
    dma = pltpu.SemaphoreType.DMA
    low = jnp.bfloat16
    return pl.pallas_call(
        up_kernel,
        out_shape=jax.ShapeDtypeStruct((2, finals, width // finals, BLK), low),
        in_specs=[pl.BlockSpec(memory_space=pltpu.SMEM), vmem, vmem, anywhere, anywhere],
        out_specs=vmem,
        scratch_shapes=[
            pltpu.VMEM((coupled, rows), low),
            pltpu.VMEM((chunks, CHUNK, width), low),
            pltpu.VMEM((2, per, BLK, BLK), low),
            pltpu.VMEM((per, BLK, BLK), low),
            pltpu.VMEM((per, BLK, BLK), low),
            pltpu.VMEM((per, BLK, BLK), low),
            pltpu.VMEM((BLK, coupled), low),
            pltpu.VMEM((BLK, width), jnp.float32),
            pltpu.VMEM((finals, width // finals, BLK), low),
            pltpu.VMEM((finals, width // finals, BLK), low),
            pltpu.VMEM((chunks, CHUNK, BLK), low),
        ]
        + plane_scratch(chunks, False)
        + [dma((2, 4, per)), dma((5, finals)), dma, dma((chunks,))],
        compiler_params=pltpu.CompilerParams(
            collective_id=cid, has_side_effects=True, vmem_limit_bytes=VMEM
        ),
    )(pick_idx, rows_low, child_low, coupling, child_inverse)


def index_kernel(map_ref, place_ref, pick_ref):
    blocks = place_ref.shape[1]
    per = pick_ref.shape[0] // 2
    first = lax.axis_index("row") * blocks
    own = lax.axis_index("col") * per

    def clear(j, _):
        for k in range(2):
            place_ref[k, j] = -1
        return 0

    lax.fori_loop(0, blocks, clear, 0, unroll=8)

    def mark(i, _):
        for k in range(2):
            at = map_ref[k, i] - first

            @pl.when((at >= 0) & (at < blocks))
            def _():
                place_ref[k, at] = i

        return 0

    lax.fori_loop(0, map_ref.shape[1], mark, 0, unroll=4)
    for k in range(2):
        for q in range(per):
            at = map_ref[k, own + q] - first
            pick_ref[k * per + q] = jnp.where((at >= 0) & (at < blocks), at, -1)


def finish_kernel(x_ref, rows_ref, o_ref, root_ref, own_ref, sem):
    own = own_ref.shape[0]
    copy = pltpu.make_async_copy(
        rows_ref.at[pl.ds(pl.multiple_of(lax.axis_index("col") * own, own), own)], own_ref, sem
    )
    copy.start()
    step = 64

    def body(i, _):
        rows = pl.ds(pl.multiple_of(i * step, step), step)
        for k in range(2):
            o_ref[rows, k, :] = x_ref[k, rows, :].astype(jnp.float32)
        return 0

    lax.fori_loop(0, o_ref.shape[0] // step, body, 0, unroll=4)
    copy.wait()
    root_ref[...] = own_ref[...].astype(jnp.float32)


def local(row_devices, col_devices, child_inverse, root_upper, coupling, child_rhs, root_rhs, child_map):
    row_place = lax.axis_index("row")
    col_place = lax.axis_index("col")
    child_slot = row_place // (row_devices // 2)
    root_rows = root_upper.shape[0]
    coupled = coupling.shape[0]
    rhs_width = child_rhs.shape[2]
    vmem = pl.BlockSpec(memory_space=pltpu.VMEM)
    smem = pl.BlockSpec(memory_space=pltpu.SMEM)
    row_bits = list(range(bits_of(row_devices)))
    col_bits = list(range(bits_of(col_devices)))
    col_orders = [col_bits, col_bits[:1] + col_bits[:0:-1]] * 2
    row_orders = [row_bits, row_bits[::-1]] * 2
    pick_order = [row_bits[-1:] + row_bits[:-1]]
    contract_first = (((0,), (0,)), ((), ()))

    per_col = coupled // BLK
    root_blocks = root_rows // BLK
    local_map = lax.dynamic_slice_in_dim(child_map, col_place * per_col, per_col, 1)
    target = local_map - row_place * root_blocks
    block_hits = target[:, :, None] == jnp.arange(root_blocks, dtype=jnp.int32)[None, None, :]
    slots = jnp.arange(2 * per_col, dtype=jnp.int32).reshape(2, per_col, 1)
    place_idx = jnp.max(jnp.where(block_hits, slots, -1), axis=1)
    pick_idx = jnp.where((target >= 0) & (target < root_blocks), target, -1).reshape(-1)
    rhs_rows = root_rhs.shape[0]
    given_rows = lax.dynamic_update_slice(
        jnp.zeros((root_rows, rhs_width), jnp.float32),
        root_rhs,
        (col_place * rhs_rows, jnp.int32(0)),
    )

    own_rhs = lax.dynamic_index_in_dim(child_rhs, child_slot, 1, keepdims=False).astype(
        jnp.bfloat16
    )
    child_low = all_sum(
        jnp.dot(child_inverse, own_rhs, preferred_element_type=jnp.float32).astype(jnp.bfloat16),
        "col", col_devices, col_orders, 0,
    )
    update = jnp.dot(coupling, child_low, preferred_element_type=jnp.float32)
    update_both = both_sum(update.astype(jnp.bfloat16), "row", row_devices, 2, 1)
    root_term = pl.pallas_call(
        place_kernel,
        out_shape=jax.ShapeDtypeStruct((root_blocks, BLK, rhs_width), jnp.bfloat16),
        in_specs=[smem, vmem, vmem],
        out_specs=vmem,
    )(
        place_idx,
        update_both.reshape(2 * per_col, BLK, rhs_width),
        given_rows.reshape(root_blocks, BLK, rhs_width),
    )
    root_low = all_sum(
        root_term.reshape(root_rows, rhs_width), "col", col_devices, col_orders, 2
    )
    solved_low = all_sum(
        lax.dot_general(
            root_upper, root_low, contract_first, preferred_element_type=jnp.float32
        ).astype(jnp.bfloat16),
        "row", row_devices, row_orders, 3,
    )
    rows_low = all_sum(
        jnp.dot(root_upper, solved_low, preferred_element_type=jnp.float32).astype(jnp.bfloat16),
        "col", col_devices, col_orders, 4,
    )
    root_solution = lax.dynamic_slice_in_dim(rows_low, col_place * rhs_rows, rhs_rows, 0).astype(
        jnp.float32
    )
    picked = pl.pallas_call(
        pick_kernel,
        out_shape=jax.ShapeDtypeStruct((2 * per_col, BLK, rhs_width), jnp.bfloat16),
        in_specs=[smem, vmem],
        out_specs=vmem,
    )(pick_idx, rows_low.reshape(root_blocks, BLK, rhs_width))
    picked_half = all_sum(
        picked.reshape(2 * coupled, rhs_width), "row", row_devices, pick_order, 5,
        gathers=len(row_bits) - 1,
    )
    own_pick = lax.dynamic_slice_in_dim(picked_half, child_slot * coupled, coupled, 0)
    back_term = all_sum(
        lax.dot_general(
            coupling, own_pick, contract_first, preferred_element_type=jnp.float32
        ).astype(jnp.bfloat16),
        "col", col_devices, col_orders, 6,
    )
    adjusted = (child_low.astype(jnp.float32) - back_term.astype(jnp.float32)).astype(
        jnp.bfloat16
    )
    final_rows = lax.dot_general(
        child_inverse, adjusted, contract_first, preferred_element_type=jnp.float32
    )
    final_both = both_sum(final_rows.astype(jnp.bfloat16), "row", row_devices, 4, 7)
    child_solution = pl.pallas_call(
        weave_kernel,
        out_shape=jax.ShapeDtypeStruct(child_rhs.shape, jnp.float32),
        in_specs=[vmem],
        out_specs=vmem,
    )(final_both)
    return (root_solution, child_solution)


def near(row_devices, col_devices, child_inverse, root_upper, coupling, child_rhs, root_rhs, child_map):
    root_rows = root_upper.shape[0]
    coupled = coupling.shape[0]
    rhs_width = child_rhs.shape[2]
    vmem = pl.BlockSpec(memory_space=pltpu.VMEM)

    per_col = coupled // BLK
    root_blocks = root_rows // BLK
    smem = pl.BlockSpec(memory_space=pltpu.SMEM)
    place_idx, pick_idx = pl.pallas_call(
        index_kernel,
        out_shape=(
            jax.ShapeDtypeStruct((2, root_blocks), jnp.int32),
            jax.ShapeDtypeStruct((2 * per_col,), jnp.int32),
        ),
        in_specs=[smem],
        out_specs=(smem, smem),
    )(child_map)
    child_low, update, given = down(child_inverse, coupling, child_rhs, root_rhs, 0)
    rows_low = root_part(place_idx, update, given, root_upper, 1)
    both = up_part(
        pick_idx, rows_low.reshape(root_blocks, BLK, rhs_width), child_low, coupling,
        child_inverse, 2,
    )
    anywhere = pl.BlockSpec(memory_space=pl.ANY)
    child_solution, root_solution = pl.pallas_call(
        finish_kernel,
        out_shape=(
            jax.ShapeDtypeStruct(child_rhs.shape, jnp.float32),
            jax.ShapeDtypeStruct(root_rhs.shape, jnp.float32),
        ),
        in_specs=[vmem, anywhere],
        out_specs=(vmem, vmem),
        scratch_shapes=[
            pltpu.VMEM(root_rhs.shape, jnp.bfloat16), pltpu.SemaphoreType.DMA,
        ],
    )(both.reshape(2, -1, rhs_width), rows_low.reshape(-1, rhs_width))
    return (root_solution, child_solution)


def solution(mesh):
    body = near if (mesh.shape["row"], mesh.shape["col"]) == (4, 8) else local
    return jax.shard_map(
        functools.partial(body, mesh.shape["row"], mesh.shape["col"]),
        mesh=mesh,
        in_specs=(
            P("row", "col"),
            P("row", "col"),
            P("col", "row"),
            P("col", None, None),
            P(("row", "col"), None),
            P(),
        ),
        out_specs=(P(("row", "col"), None), P("col", None, None)),
        check_vma=False,
    )
```
